128 devices in a mesh: ctx: 8 (over y, core), tp: 8 (over x_lo, z), pp: 2 (over x_hi).
Axes of the slice: x: 4 (x_hi: 2, x_lo: 2; x = x_hi * 2 + x_lo), y: 4, z: 4, core: 2. Of those that a mesh axis runs over, the one named last changes fastest.
Arguments:
- queries: bfloat16 [2, 2048, 12288], P('pp', 'ctx', 'tp'), may hold values from -8 to 8
- latents: bfloat16 [2, 2048, 576], P('pp', ('ctx', 'tp')), may hold values from -8 to 8
- latent_gain: float32 [2, 512], P('pp'), may hold values from 0.5 to 2
- w_ukv: bfloat16 [2, 512, 16384], P('pp', None, 'tp'), may hold values from -0.25 to 0.25
- w_o: bfloat16 [2, 8192, 7168], P('pp', 'tp'), may hold values from -0.1875 to 0.1875
- residual: bfloat16 [2, 2048, 7168], P('pp', ('ctx', 'tp')), may hold values from -3 to 3
- block_order: int32 [2, 16], P('pp'), may hold values from 0 to 15, each once within a row
Outputs:
- handed: bfloat16 [2, 2048, 7168], P('pp', ('ctx', 'tp'))
The draws below stay inside these ranges and needn't reach their ends.
Inputs may be any that keep to these rules, and one draw needn't show every extreme that they name: `block_order`: each row names each of the 16 sequence blocks once.
All inputs are finite; a program needn't handle non-finite values.
Results may differ from the reference program's by a relative error of at most 0.02.
Values may be sent and summed in bfloat16 or wider, within the bound.
A program may use at most 128 MiB of HBM per device.

```python
import math
import jax
import jax.numpy as jnp
from jax import lax

D = 7168
HEADS = 64
NOPE = 128
ROPE = 64
VDIM = 128
LATENT = 512
TOKENS = 2048
BLOCKS = 16
BLOCK_LEN = 128
SEGMENTS = 2


def latent_table(key):
    base = jax.random.fold_in(key, 101)
    keys = jax.random.split(base, 4)
    row_scale = jnp.exp(jax.random.uniform(keys[0], (SEGMENTS, TOKENS, 1), minval=math.log(0.3), maxval=math.log(3.0)))
    col_scale = jnp.exp(jax.random.uniform(keys[1], (SEGMENTS, 1, LATENT), minval=math.log(0.3), maxval=math.log(3.0)))
    compressed = jax.random.normal(keys[2], (SEGMENTS, TOKENS, LATENT)) * row_scale * col_scale
    compressed = jnp.clip(compressed, -8.0, 8.0)
    rope_raw = jnp.clip(jax.random.normal(keys[3], (SEGMENTS, TOKENS, ROPE)), -8.0, 8.0)
    return (compressed, rope_raw)


def draw_latents(key, part):
    compressed, rope_raw = latent_table(key)
    return jnp.concatenate([compressed, rope_raw], axis=-1).astype(jnp.bfloat16)


def draw_queries(key, part):
    base = jax.random.fold_in(key, 202)
    drawn = jnp.clip(jax.random.normal(base, (SEGMENTS, TOKENS, HEADS, NOPE + ROPE)), -8.0, 8.0)
    return drawn.reshape(SEGMENTS, TOKENS, HEADS * (NOPE + ROPE)).astype(jnp.bfloat16)


def levels(rng, dims, shards, smallest, high):
    level = 1.0
    for dim, parts in shards:
        heights = jax.random.uniform(jax.random.fold_in(jax.random.fold_in(rng, 6), dim), (parts,), jnp.float32, smallest / len(shards), high / len(shards))
        level = level * jnp.repeat(jnp.exp(heights), dims[dim] // parts).reshape((-1,) + (1,) * (len(dims) - 1 - dim))
    return level


def noise(rng, dims, spread, reach, pieces=(), kind=jnp.bfloat16):
    values = jax.random.normal(rng, dims, jnp.float32) * spread
    if len(pieces) > 0:
        values = levels(rng, dims, pieces, -0.22, 0.18) * values
    return jnp.clip(values, min=-reach, max=reach).astype(kind)


def setup_inputs(seed: int = 0) -> dict:
    key_list = jax.random.split(jax.random.key(seed), 8)
    queries = draw_queries(jax.random.fold_in(key_list[7], 71), 0)
    latents = draw_latents(jax.random.fold_in(key_list[7], 71), 0)
    latent_gain = jnp.clip(jnp.exp(math.log(2.0) - 1.3862944 * jax.random.uniform(key_list[2], (SEGMENTS, LATENT), jnp.float32) ** levels(key_list[2], (SEGMENTS, LATENT), ((0, 2),), -0.2, 0.2)), 0.5, 2.0)
    w_ukv = noise(key_list[3], (SEGMENTS, LATENT, HEADS * (NOPE + VDIM)), LATENT ** -0.5, 0.25, ((0, 2), (2, 8)))
    w_o = noise(key_list[4], (SEGMENTS, HEADS * VDIM, D), (HEADS * VDIM // 8) ** -0.5, 0.1875, ((0, 2), (1, 8)))
    residual = noise(key_list[5], (SEGMENTS, TOKENS, D), 0.5, 3.0, ((0, 2), (1, 64)))
    block_order = jax.vmap(lambda own: jax.random.permutation(own, BLOCKS))(jax.random.split(key_list[6], SEGMENTS)).reshape((SEGMENTS, BLOCKS)).astype(jnp.int32)
    return dict(queries=queries, latents=latents, latent_gain=latent_gain, w_ukv=w_ukv, w_o=w_o, residual=residual, block_order=block_order)


score_scale = 0.135

def rotate(values, places):
    middle = values.shape[-1] // 2
    freqs = 10000.0 ** (-(jnp.arange(middle).astype(jnp.float32) * 2.0 / values.shape[-1]))
    angles = places[..., None] * freqs
    first_half = values[..., :middle]
    second_half = values[..., middle:]
    return jnp.concatenate([first_half * jnp.cos(angles) - second_half * jnp.sin(angles), first_half * jnp.sin(angles) + second_half * jnp.cos(angles)], axis=-1)

def reference(queries, latents, latent_gain, w_ukv, w_o, residual, block_order):
    outputs = []
    for segment in range(SEGMENTS):
        row_ids = jnp.arange(TOKENS, dtype=jnp.int32)
        places = block_order[segment][row_ids // BLOCK_LEN] * BLOCK_LEN + row_ids % BLOCK_LEN
        angles_at = places.astype(jnp.float32)
        latent_rows = latents[segment].astype(jnp.float32)
        compressed = latent_rows[:, :LATENT]
        scale_rows = lax.rsqrt(lax.optimization_barrier(jnp.mean(compressed * compressed, axis=-1, keepdims=True)) + 1e-06)
        normed = (compressed * scale_rows * latent_gain[segment][None, :]).astype(jnp.bfloat16)
        key_rope = rotate(latent_rows[:, LATENT:], angles_at).astype(jnp.bfloat16)
        query_all = queries[segment].reshape(TOKENS, HEADS, NOPE + ROPE)
        query_nope = jnp.moveaxis(query_all[..., :NOPE], 1, 0)
        query_rope = jnp.moveaxis(rotate(query_all[..., NOPE:].astype(jnp.float32), angles_at[:, None]).astype(jnp.bfloat16), 1, 0)
        head_weights = jnp.moveaxis(w_ukv[segment].reshape(LATENT, HEADS, NOPE + VDIM), 1, 0)
        allowed = places[None, :] <= places[:, None]

        def one_head(inputs):
            weight_head, nope_part, rope_part = inputs
            key_value = jnp.dot(normed, weight_head, preferred_element_type=jnp.float32).astype(jnp.bfloat16)
            scores = (jnp.dot(nope_part, key_value[:, :NOPE].T, preferred_element_type=jnp.float32) + jnp.dot(rope_part, key_rope.T, preferred_element_type=jnp.float32)) * score_scale
            scores = jnp.where(allowed, scores, -1e+30)
            row_top = lax.optimization_barrier(jnp.max(scores, axis=-1, keepdims=True))
            weights = jnp.where(allowed, jnp.exp(scores - row_top), 0.0)
            totals = lax.optimization_barrier(jnp.sum(weights, axis=-1, keepdims=True))
            summed = jnp.dot(weights.astype(jnp.bfloat16), key_value[:, NOPE:], preferred_element_type=jnp.float32)
            return (summed / totals).astype(jnp.bfloat16)
        heads_out = lax.map(one_head, (head_weights, query_nope, query_rope))
        attention = jnp.moveaxis(heads_out, 0, 1).reshape(TOKENS, HEADS * VDIM)
        projected = jnp.dot(attention, w_o[segment], preferred_element_type=jnp.float32)
        outputs.append((projected + residual[segment].astype(jnp.float32)).astype(jnp.bfloat16))
    return jnp.roll(jnp.stack(outputs), 1, axis=0)
```

```python
import functools
import math

import jax
import jax.numpy as jnp
import numpy as np
from jax import lax
from jax.experimental import pallas as pl
from jax.experimental.pallas import tpu as pltpu
from jax.sharding import PartitionSpec as P

NOPE = 128
ROPE = 64
VDIM = 128
LATENT = 512
BLOCK = 128
HEADS_HERE = 8
ROWS = 256
KEYS = 2048
LATROWS = 32
D = 7168
KW = LATENT + 128
PIECE = 1024
HALF = PIECE // 2
PIECES = ("z", "x", "z", "x", "z", "x", "z")
SCALE2 = 0.135 * math.log2(math.e)

MESH = pl.DeviceIdType.MESH


def position():
    c = lax.axis_index("ctx")
    t = lax.axis_index("tp")
    p = lax.axis_index("pp")
    return c // 2, lax.rem(c, 2), t // 4, lax.rem(t, 4), p


def device(y, k, a, z, p):
    return (y * 2 + k, a * 4 + z, p)


def turn(v, n):
    return lax.rem(v + n, 4)


def rope_tables():
    f = 10000.0 ** (-(np.arange(32, dtype=np.float64) * 2.0 / ROPE))
    lane_f = np.tile(f, 4)
    sign = np.tile(np.concatenate([-np.ones(32), np.ones(32)]), 2)
    inner = np.arange(BLOCK, dtype=np.float64)[:, None] * lane_f
    outer = np.arange(16, dtype=np.float64)[:, None] * BLOCK * lane_f
    within = np.stack([np.cos(inner), np.sin(inner) * sign]).astype(np.float32)
    blocks = np.stack([np.cos(outer), np.sin(outer) * sign]).astype(np.float32)
    return within, blocks


def rotation(within, blocks, which, first, count):
    c_in = within[0, pl.ds(first, count), :]
    s_in = within[1, pl.ds(first, count), :]
    c_out = blocks[0, pl.ds(which, 1), :]
    s_out = blocks[1, pl.ds(which, 1), :]
    return c_out * c_in - s_out * s_in, s_out * c_in + c_out * s_in


def swapped(v):
    return jnp.concatenate([v[:, 32:64], v[:, :32], v[:, 96:], v[:, 64:96]], axis=1)


def remote(src, dst, send, recv, to):
    return pltpu.make_async_remote_copy(
        src_ref=src, dst_ref=dst, send_sem=send, recv_sem=recv, device_id=to, device_id_type=MESH
    )


def gather_kernel(order, lat, gain, q, within, blocks, kl, qcat, send, recv):
    y, k, a, z, p = position()
    c = y * 2 + k
    z_to = [device(y, k, a, turn(z, n), p) for n in (1, 3, 2)]
    y_to = [device(turn(y, n), k, a, z, p) for n in (1, 3, 2)]
    x_to = device(y, k, 1 - a, z, p)
    k_to = device(y, 1 - k, a, z, p)
    barrier = pltpu.get_barrier_semaphore()
    for to in z_to + y_to + [x_to, k_to]:
        pl.semaphore_signal(barrier, inc=1, device_id=to, device_id_type=MESH)

    rows = lat[0].astype(jnp.float32)
    part = rows[:, :LATENT]
    scale = lax.rsqrt(jnp.mean(part * part, axis=-1, keepdims=True) + 1e-6)
    normed = (part * scale * gain[...]).astype(jnp.bfloat16)
    tail = rows[:, LATENT:]
    twice = jnp.concatenate([tail, tail], axis=1)
    cos, sin = rotation(within, blocks, order[0, c * 2 + a], z * LATROWS, LATROWS)
    roped = (twice * cos + swapped(twice) * sin).astype(jnp.bfloat16)
    own = jnp.concatenate([normed, roped], axis=1)
    kl[0, y, k, a, z] = own[:16]
    kl[1, y, k, a, z] = own[16:]
    pl.semaphore_wait(barrier, 8)

    def copy(view, to, n):
        made = remote(view, view, send.at[n], recv.at[n], to)
        made.start()
        return made

    first = copy(kl.at[:, y, k, a, z], x_to, 0)

    places = [order[0, c * 2], order[0, c * 2 + 1]]
    lane = lax.broadcasted_iota(jnp.int32, (BLOCK, 128), 1)
    for half in range(2):
        cos, sin = rotation(within, blocks, places[half], 0, BLOCK)
        at = pl.ds(half * BLOCK, BLOCK)
        for pair in range(HEADS_HERE // 2):
            both = q[0, at, pair * 384 : (pair + 1) * 384].astype(jnp.float32)
            v = jnp.concatenate([both[:, 128:192], both[:, 320:384]], axis=1)
            turned = v * cos + swapped(v) * sin
            low = jnp.where(lane < ROPE, turned, 0.0)
            high = jnp.where(lane < ROPE, 0.0, turned)
            qcat[pair * 2, at, :] = jnp.concatenate([both[:, :128], low], axis=1).astype(jnp.bfloat16)
            qcat[pair * 2 + 1, at, :] = jnp.concatenate([both[:, 192:320], high], axis=1).astype(
                jnp.bfloat16
            )

    first.wait_recv()
    second = [copy(kl.at[0, y, k, :, z], to, 1 + i) for i, to in enumerate(z_to)]
    second += [copy(kl.at[1, y, k, :, z], to, 4 + i) for i, to in enumerate(y_to)]
    for made in second[:3]:
        made.wait_recv()
    third = [copy(kl.at[0, y, k], to, 7 + i) for i, to in enumerate(y_to)]
    for made in second[3:]:
        made.wait_recv()
    third += [copy(kl.at[1, :, k, :, z], to, 10 + i) for i, to in enumerate(z_to)]
    over = [copy(kl.at[0, y, k], k_to, 13), copy(kl.at[1, :, k, :, z], k_to, 14)]
    for i, n in enumerate((3, 1, 2)):
        third[i].wait_recv()
        over.append(copy(kl.at[0, turn(y, n), k], k_to, 15 + i))
        third[3 + i].wait_recv()
        over.append(copy(kl.at[1, :, k, :, turn(z, n)], k_to, 18 + i))
    for made in over:
        made.wait_recv()
    for made in [first] + second + third + over:
        made.wait_send()


def gather(latents, gain, queries, order):
    within, blocks = rope_tables()
    vmem = pl.BlockSpec(memory_space=pltpu.VMEM)
    return pl.pallas_call(
        gather_kernel,
        out_shape=[
            jax.ShapeDtypeStruct((2, 4, 2, 2, 4, 16, KW), jnp.bfloat16),
            jax.ShapeDtypeStruct((HEADS_HERE, ROWS, 256), jnp.bfloat16),
        ],
        in_specs=[pl.BlockSpec(memory_space=pltpu.SMEM)] + [vmem] * 5,
        out_specs=[vmem, vmem],
        scratch_shapes=[pltpu.SemaphoreType.DMA((21,)), pltpu.SemaphoreType.DMA((21,))],
        compiler_params=pltpu.CompilerParams(
            collective_id=0, has_side_effects=True, vmem_limit_bytes=24 * 2**20
        ),
        name="gather",
    )(order, latents, gain, queries, jnp.asarray(within), jnp.asarray(blocks))


def attend_kernel(order, kl, qcat, w, out):
    c = lax.axis_index("ctx")
    spot = lax.broadcasted_iota(jnp.int32, (1, 128), 1)
    inside = (lax.rem(spot, 64) // 16) * 32 + lax.rem(spot, 16)
    groups = []
    for half in range(2):
        for pair in range(8):
            base = jnp.where(spot < 64, order[0, pair * 2], order[0, pair * 2 + 1])
            groups.append(base * BLOCK + half * 16 + inside)
    key_at = jnp.concatenate(groups, axis=1)
    row = lax.broadcasted_iota(jnp.int32, (ROWS, 1), 0)
    base = jnp.where(row < BLOCK, order[0, c * 2], order[0, c * 2 + 1])
    query_at = base * BLOCK + lax.rem(row, BLOCK)
    allowed = key_at <= query_at
    for h in range(2):
        kv = jnp.dot(
            kl[:, :LATENT], w[0, :, h * 256 : (h + 1) * 256], preferred_element_type=jnp.float32
        ).astype(jnp.bfloat16)
        key = jnp.concatenate([kv[:, :NOPE], kl[:, LATENT:]], axis=1)
        scores = lax.dot_general(
            qcat[h], key, (((1,), (1,)), ((), ())), preferred_element_type=jnp.float32
        )
        scores = jnp.where(allowed, scores * SCALE2, -1e30)
        top = jnp.max(scores, axis=-1, keepdims=True)
        weights = jnp.exp2(scores - top)
        total = jnp.sum(weights, axis=-1, keepdims=True)
        summed = jnp.dot(
            weights.astype(jnp.bfloat16), kv[:, NOPE:], preferred_element_type=jnp.float32
        )
        out[:, h * VDIM : (h + 1) * VDIM] = (summed / total).astype(jnp.bfloat16)


def attend(order, kl, qcat, w):
    return pl.pallas_call(
        attend_kernel,
        grid=(HEADS_HERE // 2,),
        out_shape=jax.ShapeDtypeStruct((ROWS, HEADS_HERE * VDIM), jnp.bfloat16),
        in_specs=[
            pl.BlockSpec(memory_space=pltpu.SMEM),
            pl.BlockSpec((KEYS, KW), lambda i: (0, 0)),
            pl.BlockSpec((2, ROWS, 256), lambda i: (i, 0, 0)),
            pl.BlockSpec((1, LATENT, 512), lambda i: (0, 0, i)),
        ],
        out_specs=pl.BlockSpec((ROWS, 2 * VDIM), lambda i: (0, i)),
        compiler_params=pltpu.CompilerParams(vmem_limit_bytes=40 * 2**20),
        name="attend",
    )(order, kl.reshape(KEYS, KW), qcat, w)


def project_kernel(att, w, residual, out, wv, part, early, late, crossed, final, wsem, send, recv):
    y, k, a, z, p = position()
    up, down, far = turn(z, 1), turn(z, 3), turn(z, 2)
    to_up, to_down = device(y, k, a, up, p), device(y, k, a, down, p)
    to_x = device(y, k, 1 - a, z, p)
    to_pp = device(y, k, 1 - a, z, 1 - p)
    barrier = pltpu.get_barrier_semaphore()
    for to in (to_up, to_down, to_x, to_pp):
        pl.semaphore_signal(barrier, inc=1, device_id=to, device_id_type=MESH)
    columns = [pl.ds(j * PIECE, PIECE) for j in range(len(PIECES))]
    loads = []
    for j in range(len(PIECES)):
        load = pltpu.make_async_copy(w.at[0, :, columns[j]], wv.at[j], wsem.at[j])
        load.start()
        loads.append(load)
    left, right = pl.ds(0, HALF), pl.ds(HALF, HALF)
    sent = []
    copies = {}

    def copy(src, dst, j, n, to):
        made = remote(src, dst, send.at[j, n], recv.at[j, n], to)
        made.start()
        sent.append(made)
        copies[j, n] = made

    def wide(ref):
        return ref[...].astype(jnp.float32)

    def own_residual(j):
        return residual[0, :, columns[j]].astype(jnp.float32)

    def spread(j, side):
        copy(part.at[j, side, far, :, left], early.at[j, 0, side], j, 0, to_up)
        copy(part.at[j, side, far, :, right], early.at[j, 1, side], j, 1, to_down)
        copy(part.at[j, side, up, :, right], late.at[j, 0, side, :, right], j, 2, to_up)
        copy(part.at[j, side, down, :, left], late.at[j, 1, side, :, left], j, 3, to_down)

    def relay(j, side):
        copies[j, 0].wait_recv()
        mine = part.at[j, side, up, :, left]
        mine[...] = (wide(mine) + wide(early.at[j, 0, side])).astype(jnp.bfloat16)
        copy(mine, late.at[j, 0, side, :, left], j, 4, to_up)
        copies[j, 1].wait_recv()
        mine = part.at[j, side, down, :, right]
        mine[...] = (wide(mine) + wide(early.at[j, 1, side])).astype(jnp.bfloat16)
        copy(mine, late.at[j, 1, side, :, right], j, 5, to_down)

    def landed(j):
        for n in (2, 3, 4, 5):
            copies[j, n].wait_recv()

    def ring_sum(j, side):
        return wide(part.at[j, side, z]) + wide(late.at[j, 0, side]) + wide(late.at[j, 1, side])

    def finish(j, value):
        final[j] = value.astype(jnp.bfloat16)
        copy(final.at[j], out.at[0, :, columns[j]], j, 7, to_pp)

    def product(j):
        loads[j].wait()
        made = jnp.dot(att[...], wv[j], preferred_element_type=jnp.float32)
        part[j] = made.astype(jnp.bfloat16).reshape(2, 4, LATROWS, PIECE)

    def z_step(j, step):
        if step == 0:
            product(j)
            if j == 0:
                pl.semaphore_wait(barrier, 4)
            spread(j, slice(None))
        elif step == 1:
            relay(j, slice(None))
        elif step == 2:
            landed(j)
            part[j, a, z] = (ring_sum(j, a) + own_residual(j)).astype(jnp.bfloat16)
            copy(part.at[j, a, z], crossed.at[j, 0], j, 6, to_x)
        elif step == 3:
            copies[j, 6].wait_recv()
            finish(j, ring_sum(j, 1 - a) + wide(crossed.at[j, 0]))

    def x_step(j, step):
        if step == 0:
            product(j)
            part[j, a, z] = (wide(part.at[j, a, z]) + own_residual(j)).astype(jnp.bfloat16)
            copy(part.at[j, a], crossed.at[j], j, 6, to_x)
        elif step == 1:
            copies[j, 6].wait_recv()
            part[j, 1 - a] = (wide(part.at[j, 1 - a]) + wide(crossed.at[j])).astype(jnp.bfloat16)
            spread(j, 1 - a)
        elif step == 2:
            relay(j, 1 - a)
        elif step == 3:
            landed(j)
            finish(j, ring_sum(j, 1 - a))

    steps = {"z": z_step, "x": x_step}
    for step in range(len(PIECES) + 3):
        for j, kind in enumerate(PIECES):
            if 0 <= step - j < 4:
                steps[kind](j, step - j)
    for j in range(len(PIECES)):
        copies[j, 7].wait_recv()
    for made in sent:
        made.wait_send()


def project(att, w_o, residual):
    n = len(PIECES)
    vmem = pl.BlockSpec(memory_space=pltpu.VMEM)
    return pl.pallas_call(
        project_kernel,
        out_shape=jax.ShapeDtypeStruct((1, LATROWS, D), jnp.bfloat16),
        in_specs=[vmem, pl.BlockSpec(memory_space=pl.ANY), vmem],
        out_specs=vmem,
        scratch_shapes=[
            pltpu.VMEM((n, HEADS_HERE * VDIM, PIECE), jnp.bfloat16),
            pltpu.VMEM((n, 2, 4, LATROWS, PIECE), jnp.bfloat16),
            pltpu.VMEM((n, 2, 2, LATROWS, HALF), jnp.bfloat16),
            pltpu.VMEM((n, 2, 2, LATROWS, PIECE), jnp.bfloat16),
            pltpu.VMEM((n, 4, LATROWS, PIECE), jnp.bfloat16),
            pltpu.VMEM((n, LATROWS, PIECE), jnp.bfloat16),
            pltpu.SemaphoreType.DMA((n,)),
            pltpu.SemaphoreType.DMA((n, 8)),
            pltpu.SemaphoreType.DMA((n, 8)),
        ],
        compiler_params=pltpu.CompilerParams(
            collective_id=1, has_side_effects=True, vmem_limit_bytes=48 * 2**20
        ),
        name="project",
    )(att, w_o, residual)


def local(queries, latents, latent_gain, w_ukv, w_o, residual, block_order):
    kl, qcat = gather(latents, latent_gain, queries, block_order)
    att = attend(block_order, kl, qcat, w_ukv)
    return project(att, w_o, residual)


def solution(mesh):
    in_specs = (
        P("pp", "ctx", "tp"),
        P("pp", ("ctx", "tp"), None),
        P("pp", None),
        P("pp", None, "tp"),
        P("pp", "tp", None),
        P("pp", ("ctx", "tp"), None),
        P("pp", None),
    )
    out_specs = P("pp", ("ctx", "tp"), None)
    return jax.shard_map(local, mesh=mesh, in_specs=in_specs, out_specs=out_specs, check_vma=False)
```

```python
import math

import jax
import jax.numpy as jnp
import numpy as np
from jax import lax
from jax.experimental import pallas as pl
from jax.experimental.pallas import tpu as pltpu
from jax.sharding import PartitionSpec as P

NOPE = 128
ROPE = 64
VDIM = 128
LATENT = 512
BLOCK = 128
HEADS = 8
ROWS = 256
LATROWS = 32
D = 7168
KW = LATENT + 128
CHUNK = 512
PIECE = 1024
HALF = PIECE // 2
PIECES = ("z", "x", "z", "x", "z", "x", "z")
SCALE2 = 0.135 * math.log2(math.e)

MESH = pl.DeviceIdType.MESH


def device(y, k, a, z, p):
    return (y * 2 + k, a * 4 + z, p)


def turn(v, n):
    return lax.rem(v + n, 4)


def rope_tables():
    f = 10000.0 ** (-(np.arange(32, dtype=np.float64) * 2.0 / ROPE))
    lane_f = np.tile(f, 4)
    sign = np.tile(np.concatenate([-np.ones(32), np.ones(32)]), 2)
    inner = np.arange(BLOCK, dtype=np.float64)[:, None] * lane_f
    outer = np.arange(16, dtype=np.float64)[:, None] * BLOCK * lane_f
    within = np.stack([np.cos(inner), np.sin(inner) * sign]).astype(np.float32)
    blocks = np.stack([np.cos(outer), np.sin(outer) * sign]).astype(np.float32)
    return np.concatenate([within, blocks], axis=1)


def rotation(tables, which, first, count):
    c_in = tables[0, pl.ds(first, count), :]
    s_in = tables[1, pl.ds(first, count), :]
    c_out = tables[0, pl.ds(BLOCK + which, 1), :]
    s_out = tables[1, pl.ds(BLOCK + which, 1), :]
    return c_out * c_in - s_out * s_in, s_out * c_in + c_out * s_in


def swapped(v):
    return jnp.concatenate([v[:, 32:64], v[:, :32], v[:, 96:], v[:, 64:96]], axis=1)


def remote(src, dst, send, recv, to):
    return pltpu.make_async_remote_copy(
        src_ref=src, dst_ref=dst, send_sem=send, recv_sem=recv, device_id=to, device_id_type=MESH
    )


def wide(ref):
    return ref[...].astype(jnp.float32)


def layer_kernel(
    lat_in, gain_in, tables_in, order_in, q_in, up_in, w_in, residual_in,
    out,
    lat, gain, tables, order, q, up, wv, residual,
    kl, qcat, top, acc, att,
    part, early, late, crossed, final,
    load_sem, up_sem, w_sem, g_send, g_recv, send, recv,
):
    c = lax.axis_index("ctx")
    t = lax.axis_index("tp")
    p = lax.axis_index("pp")
    y, k, a, z = c // 2, lax.rem(c, 2), t // 4, lax.rem(t, 4)
    z_to = {n: device(y, k, a, turn(z, n), p) for n in (1, 3, 2)}
    y_to = {n: device(turn(y, n), k, a, z, p) for n in (1, 3, 2)}
    x_to = device(y, k, 1 - a, z, p)
    k_to = device(y, 1 - k, a, z, p)
    pp_to = device(y, k, 1 - a, z, 1 - p)

    barrier = pltpu.get_barrier_semaphore()
    for to in [*z_to.values(), *y_to.values(), x_to, k_to, pp_to]:
        pl.semaphore_signal(barrier, inc=1, device_id=to, device_id_type=MESH)

    loads = {}

    def load(name, src, dst, sem):
        made = pltpu.make_async_copy(src, dst, sem)
        made.start()
        loads[name] = made

    load("lat", lat_in.at[0], lat, load_sem.at[0])
    load("order", order_in, order, load_sem.at[1])
    load("gain", gain_in, gain, load_sem.at[2])
    load("tables", tables_in, tables, load_sem.at[3])
    load("q", q_in.at[0], q, load_sem.at[4])
    for h in range(HEADS):
        load(("up", h), up_in.at[0, :, pl.ds(h * 256, 256)], up.at[h], up_sem.at[h])
    columns = [pl.ds(j * PIECE, PIECE) for j in range(len(PIECES))]
    for j in range(len(PIECES)):
        load(("w", j), w_in.at[0, :, columns[j]], wv.at[j], w_sem.at[j])
    load("residual", residual_in.at[0], residual, load_sem.at[5])

    for name in ("lat", "order", "gain", "tables"):
        loads[name].wait()
    rows = lat[...].astype(jnp.float32)
    low_rank = rows[:, :LATENT]
    scale = lax.rsqrt(jnp.mean(low_rank * low_rank, axis=-1, keepdims=True) + 1e-6)
    normed = (low_rank * scale * gain[...]).astype(jnp.bfloat16)
    twice = jnp.concatenate([rows[:, LATENT:], rows[:, LATENT:]], axis=1)
    cos, sin = rotation(tables, order[0, c * 2 + a], z * LATROWS, LATROWS)
    roped = (twice * cos + swapped(twice) * sin).astype(jnp.bfloat16)
    own = jnp.concatenate([normed, roped], axis=1)
    kl[0, 0, 0, 0, 0] = own[:16]
    kl[0, 1, 0, 0, 0] = own[16:]
    pl.semaphore_wait(barrier, 9)

    sent = []

    def push(src, dst, n, to):
        made = remote(src, dst, g_send.at[n], g_recv.at[n], to)
        made.start()
        sent.append(made)
        return made

    to_x = push(kl.at[0, :, 0, 0, 0], kl.at[0, :, 0, 1, 0], 0, x_to)

    loads["q"].wait()
    lane = lax.broadcasted_iota(jnp.int32, (BLOCK, 128), 1)
    for half in range(2):
        cos, sin = rotation(tables, order[0, c * 2 + half], 0, BLOCK)
        at = pl.ds(half * BLOCK, BLOCK)
        for pair in range(HEADS // 2):
            both = q[at, pair * 384 : (pair + 1) * 384].astype(jnp.float32)
            v = jnp.concatenate([both[:, 128:192], both[:, 320:384]], axis=1)
            turned = v * cos + swapped(v) * sin
            low = jnp.where(lane < ROPE, turned, 0.0)
            high = jnp.where(lane < ROPE, 0.0, turned)
            qcat[pair * 2, at, :] = jnp.concatenate([both[:, :128], low], axis=1).astype(jnp.bfloat16)
            qcat[pair * 2 + 1, at, :] = jnp.concatenate([both[:, 192:320], high], axis=1).astype(
                jnp.bfloat16
            )

    to_x.wait_recv()
    near = []
    for i, n in enumerate((1, 3, 2)):
        near.append(push(kl.at[0, 0, 0, :, 0], kl.at[0, 0, 0, :, 4 - n], 1 + i, z_to[n]))
        near.append(push(kl.at[0, 1, 0, :, 0], kl.at[0, 1, 0, :, 4 - n], 4 + i, y_to[n]))
    for made in near:
        made.wait_recv()
    arrivals = {}
    for i, n in enumerate((3, 1, 2)):
        arrivals[4 - n] = (
            push(kl.at[0, 0, 0], kl.at[4 - n, 0, 0], 7 + i, y_to[n]),
            push(kl.at[0, 1, 0], kl.at[4 - n, 1, 0], 10 + i, z_to[n]),
        )

    def share(slot):
        return push(kl.at[slot, :, 0], kl.at[slot, :, 1], 13 + slot, k_to)

    row = lax.broadcasted_iota(jnp.int32, (ROWS, 1), 0)
    base = jnp.where(row < BLOCK, order[0, c * 2], order[0, c * 2 + 1])
    query_at = base * BLOCK + lax.rem(row, BLOCK)
    spot = lax.broadcasted_iota(jnp.int32, (1, 128), 1)
    minor = lax.rem(spot, 64) // 16
    deep = lax.rem(spot, 16)

    def key_places(slot):
        groups = []
        for core in range(2):
            there = turn(y, slot) * 2 + (k if core == 0 else 1 - k)
            block = jnp.where(spot < 64, order[0, there * 2 + a], order[0, there * 2 + 1 - a])
            groups.append(block * BLOCK + lax.rem(minor + z, 4) * LATROWS + deep)
        for core in range(2):
            block = jnp.zeros_like(spot)
            for m in range(4):
                there = turn(y, m) * 2 + (k if core == 0 else 1 - k)
                here = jnp.where(spot < 64, order[0, there * 2 + a], order[0, there * 2 + 1 - a])
                block = jnp.where(minor == m, here, block)
            groups.append(block * BLOCK + turn(z, slot) * LATROWS + 16 + deep)
        return jnp.concatenate(groups, axis=1)

    ones = jnp.ones((CHUNK, VDIM), jnp.bfloat16)

    def attend(slot, first, last):
        allowed = key_places(slot) <= query_at

        def one(h):
            latent = kl[slot].reshape(CHUNK, KW)
            kv = jnp.dot(latent[:, :LATENT], up[h], preferred_element_type=jnp.float32)
            kv = kv.astype(jnp.bfloat16)
            key = jnp.concatenate([kv[:, :NOPE], latent[:, LATENT:]], axis=1)
            scores = lax.dot_general(
                qcat[h], key, (((1,), (1,)), ((), ())), preferred_element_type=jnp.float32
            )
            scores = jnp.where(allowed, scores * SCALE2, -1e30)
            high = jnp.max(scores, axis=-1, keepdims=True)
            if not first:
                before = top[h]
                high = jnp.maximum(before[:, :1], high)
            weights = jnp.exp2(scores - high).astype(jnp.bfloat16)
            value = jnp.concatenate([kv[:, NOPE:], ones], axis=1)
            summed = jnp.dot(weights, value, preferred_element_type=jnp.float32)
            if not first:
                summed = summed + acc[h] * jnp.exp2(before[:, :1] - high)
            if last:
                att[h] = (summed[:, :VDIM] / summed[:, VDIM:]).astype(jnp.bfloat16)
            else:
                top[h] = jnp.broadcast_to(high, (ROWS, 128))
                acc[h] = summed

        @pl.loop(0, HEADS // 2)
        def _(i):
            one(i * 2)
            one(i * 2 + 1)

    def landed_slot(slot):
        for made in arrivals[slot]:
            made.wait_recv()

    shared = {0: share(0)}
    for h in range(HEADS):
        loads["up", h].wait()
    shared[0].wait_recv()
    attend(0, True, False)
    landed_slot(1)
    shared[1] = share(1)
    landed_slot(3)
    shared[3] = share(3)
    shared[1].wait_recv()
    attend(1, False, False)
    landed_slot(2)
    shared[2] = share(2)
    shared[3].wait_recv()
    attend(3, False, False)
    shared[2].wait_recv()
    attend(2, False, True)

    above, below, far = turn(z, 1), turn(z, 3), turn(z, 2)
    left, right = pl.ds(0, HALF), pl.ds(HALF, HALF)
    copies = {}

    def copy(src, dst, j, n, to):
        made = remote(src, dst, send.at[j, n], recv.at[j, n], to)
        made.start()
        sent.append(made)
        copies[j, n] = made

    def own_residual(j):
        return residual[:, columns[j]].astype(jnp.float32)

    def spread(j, side):
        copy(part.at[j, side, far, :, left], early.at[j, 0, side], j, 0, z_to[1])
        copy(part.at[j, side, far, :, right], early.at[j, 1, side], j, 1, z_to[3])
        copy(part.at[j, side, above, :, right], late.at[j, 0, side, :, right], j, 2, z_to[1])
        copy(part.at[j, side, below, :, left], late.at[j, 1, side, :, left], j, 3, z_to[3])

    def relay(j, side):
        copies[j, 0].wait_recv()
        mine = part.at[j, side, above, :, left]
        mine[...] = (wide(mine) + wide(early.at[j, 0, side])).astype(jnp.bfloat16)
        copy(mine, late.at[j, 0, side, :, left], j, 4, z_to[1])
        copies[j, 1].wait_recv()
        mine = part.at[j, side, below, :, right]
        mine[...] = (wide(mine) + wide(early.at[j, 1, side])).astype(jnp.bfloat16)
        copy(mine, late.at[j, 1, side, :, right], j, 5, z_to[3])

    def landed(j):
        for n in (2, 3, 4, 5):
            copies[j, n].wait_recv()

    def ring_sum(j, side):
        return wide(part.at[j, side, z]) + wide(late.at[j, 0, side]) + wide(late.at[j, 1, side])

    def finish(j, value):
        final[j] = value.astype(jnp.bfloat16)
        copy(final.at[j], out.at[0, :, columns[j]], j, 7, pp_to)

    def product(j):
        loads["w", j].wait()
        heads = jnp.concatenate([att[h] for h in range(HEADS)], axis=1)
        made = jnp.dot(heads, wv[j], preferred_element_type=jnp.float32)
        part[j] = made.astype(jnp.bfloat16).reshape(2, 4, LATROWS, PIECE)

    def z_step(j, step):
        if step == 0:
            product(j)
            spread(j, slice(None))
        elif step == 1:
            relay(j, slice(None))
        elif step == 2:
            landed(j)
            part[j, a, z] = (ring_sum(j, a) + own_residual(j)).astype(jnp.bfloat16)
            copy(part.at[j, a, z], crossed.at[j, 0], j, 6, x_to)
        elif step == 3:
            copies[j, 6].wait_recv()
            finish(j, ring_sum(j, 1 - a) + wide(crossed.at[j, 0]))

    def x_step(j, step):
        if step == 0:
            product(j)
            part[j, a, z] = (wide(part.at[j, a, z]) + own_residual(j)).astype(jnp.bfloat16)
            copy(part.at[j, a], crossed.at[j], j, 6, x_to)
        elif step == 1:
            copies[j, 6].wait_recv()
            part[j, 1 - a] = (wide(part.at[j, 1 - a]) + wide(crossed.at[j])).astype(jnp.bfloat16)
            spread(j, 1 - a)
        elif step == 2:
            relay(j, 1 - a)
        elif step == 3:
            landed(j)
            finish(j, ring_sum(j, 1 - a))

    steps = {"z": z_step, "x": x_step}
    loads["residual"].wait()
    for j, kind in enumerate(PIECES):
        steps[kind](j, 0)
    for step in range(1, len(PIECES) + 3):
        for j, kind in enumerate(PIECES):
            if 1 <= step - j < 4:
                steps[kind](j, step - j)
    for j in range(len(PIECES)):
        copies[j, 7].wait_recv()
    for made in sent:
        made.wait_send()


def local(queries, latents, latent_gain, w_ukv, w_o, residual, block_order):
    n = len(PIECES)
    hbm = pl.BlockSpec(memory_space=pltpu.HBM)
    bf16, f32 = jnp.bfloat16, jnp.float32
    dma = pltpu.SemaphoreType.DMA
    return pl.pallas_call(
        layer_kernel,
        out_shape=jax.ShapeDtypeStruct((1, LATROWS, D), bf16),
        in_specs=[hbm] * 8,
        out_specs=pl.BlockSpec(memory_space=pltpu.VMEM),
        scratch_shapes=[
            pltpu.VMEM((LATROWS, LATENT + ROPE), bf16),
            pltpu.VMEM((1, LATENT), f32),
            pltpu.VMEM((2, BLOCK + 16, 128), f32),
            pltpu.SMEM((1, 16), jnp.int32),
            pltpu.VMEM((ROWS, HEADS * (NOPE + ROPE)), bf16),
            pltpu.VMEM((HEADS, LATENT, 256), bf16),
            pltpu.VMEM((n, HEADS * VDIM, PIECE), bf16),
            pltpu.VMEM((LATROWS, D), bf16),
            pltpu.VMEM((4, 2, 2, 2, 4, 16, KW), bf16),
            pltpu.VMEM((HEADS, ROWS, 256), bf16),
            pltpu.VMEM((HEADS, ROWS, 128), f32),
            pltpu.VMEM((HEADS, ROWS, 256), f32),
            pltpu.VMEM((HEADS, ROWS, VDIM), bf16),
            pltpu.VMEM((n, 2, 4, LATROWS, PIECE), bf16),
            pltpu.VMEM((n, 2, 2, LATROWS, HALF), bf16),
            pltpu.VMEM((n, 2, 2, LATROWS, PIECE), bf16),
            pltpu.VMEM((n, 4, LATROWS, PIECE), bf16),
            pltpu.VMEM((n, LATROWS, PIECE), bf16),
            dma((6,)),
            dma((HEADS,)),
            dma((n,)),
            dma((17,)),
            dma((17,)),
            dma((n, 8)),
            dma((n, 8)),
        ],
        compiler_params=pltpu.CompilerParams(
            collective_id=0, has_side_effects=True, vmem_limit_bytes=58 * 2**20
        ),
        name="layer",
    )(latents, latent_gain, jnp.asarray(rope_tables()), block_order, queries, w_ukv, w_o, residual)


def solution(mesh):
    in_specs = (
        P("pp", "ctx", "tp"),
        P("pp", ("ctx", "tp"), None),
        P("pp", None),
        P("pp", None, "tp"),
        P("pp", "tp", None),
        P("pp", ("ctx", "tp"), None),
        P("pp", None),
    )
    out_specs = P("pp", ("ctx", "tp"), None)
    return jax.shard_map(local, mesh=mesh, in_specs=in_specs, out_specs=out_specs, check_vma=False)
```

```python
import math

import jax
import jax.numpy as jnp
import numpy as np
from jax import lax
from jax.experimental import pallas as pl
from jax.experimental.pallas import tpu as pltpu
from jax.sharding import PartitionSpec as P

NOPE = 128
ROPE = 64
VDIM = 128
LATENT = 512
BLOCK = 128
HEADS = 8
ROWS = 256
LATROWS = 32
D = 7168
KW = LATENT + 128
CHUNK = 512
PIECE = 1024
HALF = PIECE // 2
PIECES = ("x", "z", "x", "z", "x", "z", "z")
ORDER = (
    (1, 1), (3, 1), (0, 1), (5, 1), (6, 1), (2, 1), (1, 2), (3, 2), (0, 2), (4, 1), (5, 2),
    (1, 3), (6, 2), (3, 3), (2, 2), (0, 3), (5, 3), (4, 2), (6, 3), (2, 3), (4, 3),
)
SCALE2 = 0.135 * math.log2(math.e)

MESH = pl.DeviceIdType.MESH


def device(y, k, a, z, p):
    return (y * 2 + k, a * 4 + z, p)


def turn(v, n):
    return lax.rem(v + n, 4)


def rope_tables():
    f = 10000.0 ** (-(np.arange(32, dtype=np.float64) * 2.0 / ROPE))
    lane_f = np.tile(f, 4)
    sign = np.tile(np.concatenate([-np.ones(32), np.ones(32)]), 2)
    inner = np.arange(BLOCK, dtype=np.float64)[:, None] * lane_f
    outer = np.arange(16, dtype=np.float64)[:, None] * BLOCK * lane_f
    within = np.stack([np.cos(inner), np.sin(inner) * sign]).astype(np.float32)
    blocks = np.stack([np.cos(outer), np.sin(outer) * sign]).astype(np.float32)
    return np.concatenate([within, blocks], axis=1)


def rotation(tables, which, first, count):
    c_in = tables[0, pl.ds(first, count), :]
    s_in = tables[1, pl.ds(first, count), :]
    c_out = tables[0, pl.ds(BLOCK + which, 1), :]
    s_out = tables[1, pl.ds(BLOCK + which, 1), :]
    return c_out * c_in - s_out * s_in, s_out * c_in + c_out * s_in


def swapped(v):
    return jnp.concatenate([v[:, 32:64], v[:, :32], v[:, 96:], v[:, 64:96]], axis=1)


def remote(src, dst, send, recv, to):
    return pltpu.make_async_remote_copy(
        src_ref=src, dst_ref=dst, send_sem=send, recv_sem=recv, device_id=to, device_id_type=MESH
    )


def wide(ref):
    return ref[...].astype(jnp.float32)


def layer_kernel(
    lat_in, gain_in, tables_in, order_in, q_in, up_in, w_in, residual_in,
    out,
    lat, gain, tables, order, q, up_k, up_v, wv, residual,
    kl, q_t, up_vt, key, value_t, bias, top, acc, att,
    part, early, late, crossed, final,
    load_sem, up_sem, w_sem, g_send, g_recv, send, recv,
):
    c = lax.axis_index("ctx")
    t = lax.axis_index("tp")
    p = lax.axis_index("pp")
    y, k, a, z = c // 2, lax.rem(c, 2), t // 4, lax.rem(t, 4)
    z_to = {n: device(y, k, a, turn(z, n), p) for n in (1, 3, 2)}
    y_to = {n: device(turn(y, n), k, a, z, p) for n in (1, 3, 2)}
    x_to = device(y, k, 1 - a, z, p)
    k_to = device(y, 1 - k, a, z, p)
    pp_to = device(y, k, 1 - a, z, 1 - p)

    barrier = pltpu.get_barrier_semaphore()
    for to in [*z_to.values(), *y_to.values(), x_to, k_to, pp_to]:
        pl.semaphore_signal(barrier, inc=1, device_id=to, device_id_type=MESH)

    loads = {}

    def load(name, src, dst, sem):
        made = pltpu.make_async_copy(src, dst, sem)
        made.start()
        loads[name] = made

    load("lat", lat_in.at[0], lat, load_sem.at[0])
    load("order", order_in, order, load_sem.at[1])
    load("gain", gain_in, gain, load_sem.at[2])
    load("tables", tables_in, tables, load_sem.at[3])
    load("q", q_in.at[0], q, load_sem.at[4])
    for h in range(HEADS):
        at = pl.ds(h * VDIM, VDIM)
        load(("k", h), up_in.at[0, :, pl.ds(h * 256, NOPE)], up_k.at[:, at], up_sem.at[h])
        load(("v", h), up_in.at[0, :, pl.ds(h * 256 + NOPE, VDIM)], up_v.at[:, at], up_sem.at[8 + h])
    columns = [pl.ds(j * PIECE, PIECE) for j in range(len(PIECES))]
    for j in range(len(PIECES)):
        load(("w", j), w_in.at[0, :, columns[j]], wv.at[j], w_sem.at[j])
    load("residual", residual_in.at[0], residual, load_sem.at[5])

    for name in ("lat", "order", "gain", "tables"):
        loads[name].wait()
    rows = lat[...].astype(jnp.float32)
    low_rank = rows[:, :LATENT]
    scale = lax.rsqrt(jnp.mean(low_rank * low_rank, axis=-1, keepdims=True) + 1e-6)
    normed = (low_rank * scale * gain[...]).astype(jnp.bfloat16)
    twice = jnp.concatenate([rows[:, LATENT:], rows[:, LATENT:]], axis=1)
    cos, sin = rotation(tables, order[0, c * 2 + a], z * LATROWS, LATROWS)
    roped = ((twice * cos + swapped(twice) * sin) * SCALE2).astype(jnp.bfloat16)
    own = jnp.concatenate([normed, roped], axis=1)
    kl[0, 0, 0, 0, 0] = own[:16]
    kl[0, 1, 0, 0, 0] = own[16:]
    pl.semaphore_wait(barrier, 9)

    sent = []

    def push(src, dst, n, to):
        made = remote(src, dst, g_send.at[n], g_recv.at[n], to)
        made.start()
        sent.append(made)
        return made

    to_x = push(kl.at[0, :, 0, 0, 0], kl.at[0, :, 0, 1, 0], 0, x_to)

    loads["q"].wait()
    lane = lax.broadcasted_iota(jnp.int32, (BLOCK, 128), 1)
    for half in range(2):
        cos, sin = rotation(tables, order[0, c * 2 + half], 0, BLOCK)
        at = pl.ds(half * BLOCK, BLOCK)
        for pair in range(HEADS // 2):
            both = q[at, pair * 384 : (pair + 1) * 384].astype(jnp.float32)
            v = jnp.concatenate([both[:, 128:192], both[:, 320:384]], axis=1)
            turned = v * cos + swapped(v) * sin
            q_t[pair * 2, :NOPE, at] = both[:, :128].T.astype(jnp.bfloat16)
            q_t[pair * 2, NOPE:, at] = jnp.where(lane < ROPE, turned, 0.0).T.astype(jnp.bfloat16)
            q_t[pair * 2 + 1, :NOPE, at] = both[:, 192:320].T.astype(jnp.bfloat16)
            q_t[pair * 2 + 1, NOPE:, at] = jnp.where(lane < ROPE, 0.0, turned).T.astype(jnp.bfloat16)

    to_x.wait_recv()
    near = []
    for i, n in enumerate((1, 3, 2)):
        near.append(push(kl.at[0, 0, 0, :, 0], kl.at[0, 0, 0, :, 4 - n], 1 + i, z_to[n]))
        near.append(push(kl.at[0, 1, 0, :, 0], kl.at[0, 1, 0, :, 4 - n], 4 + i, y_to[n]))
    for h in range(HEADS):
        loads["v", h].wait()
        at = pl.ds(h * VDIM, VDIM)
        up_vt[at, :] = up_v[:, at].astype(jnp.float32).T.astype(jnp.bfloat16)
    for made in near:
        made.wait_recv()
    arrivals = {}
    for i, n in enumerate((3, 1, 2)):
        arrivals[4 - n] = (
            push(kl.at[0, 0, 0], kl.at[4 - n, 0, 0], 7 + i, y_to[n]),
            push(kl.at[0, 1, 0], kl.at[4 - n, 1, 0], 10 + i, z_to[n]),
        )

    def share(slot):
        return push(kl.at[slot, :, 0], kl.at[slot, :, 1], 13 + slot, k_to)

    row = lax.broadcasted_iota(jnp.int32, (BLOCK, BLOCK), 0)
    second = row >= 64
    minor = lax.rem(row, 64) // 16
    deep = lax.rem(row, 16)
    query_in = lax.broadcasted_iota(jnp.int32, (BLOCK, BLOCK), 1)
    query_at = [order[0, c * 2 + n] * BLOCK + query_in for n in range(2)]

    def mask(slot):
        for half in range(2):
            for core in range(2):
                here = k if core == 0 else 1 - k
                if half == 0:
                    there = (turn(y, slot) * 2 + here) * 2
                    block = jnp.where(second, order[0, there + 1 - a], order[0, there + a])
                    key_at = block * BLOCK + lax.rem(minor + z, 4) * LATROWS + deep
                else:
                    block = jnp.zeros_like(row)
                    for m in range(4):
                        there = (turn(y, m) * 2 + here) * 2
                        one = jnp.where(second, order[0, there + 1 - a], order[0, there + a])
                        block = jnp.where(minor == m, one, block)
                    key_at = block * BLOCK + turn(z, slot) * LATROWS + 16 + deep
                for n in range(2):
                    bias[pl.ds((half * 2 + core) * BLOCK, BLOCK), pl.ds(n * BLOCK, BLOCK)] = jnp.where(
                        key_at <= query_at[n], 0.0, -1e30
                    )

    ones = jnp.ones((16, CHUNK), jnp.bfloat16)

    def attend(slot, first, last, between):
        mask(slot)
        latent = kl[slot].reshape(CHUNK, KW)
        low_rank, key_rope = latent[:, :LATENT], latent[:, LATENT:]
        for n in range(4):
            at = pl.ds(n * 256, 256)
            made = jnp.dot(low_rank, up_k[:, at], preferred_element_type=jnp.float32)
            key[:, at] = (made * SCALE2).astype(jnp.bfloat16)
        for n in range(4):
            at = pl.ds(n * 256, 256)
            value_t[at, :] = lax.dot_general(
                up_vt[at, :], low_rank, (((1,), (1,)), ((), ())), preferred_element_type=jnp.float32
            ).astype(jnp.bfloat16)
        for h in range(HEADS):
            if h == 5:
                between()
            at = pl.ds(h * VDIM, VDIM)
            keys = jnp.concatenate([key[:, at], key_rope], axis=1)
            scores = jnp.dot(keys, q_t[h], preferred_element_type=jnp.float32) + bias[...]
            high = jnp.max(scores, axis=0, keepdims=True)
            if not first:
                before = top[h, :1]
                high = jnp.maximum(before, high)
            weights = jnp.exp2(scores - high).astype(jnp.bfloat16)
            values = jnp.concatenate([value_t[at, :], ones], axis=0)
            summed = jnp.dot(values, weights, preferred_element_type=jnp.float32)
            if not first:
                summed = summed + acc[h] * jnp.exp2(before - high)
            if last:
                shared_out = summed[:VDIM] / summed[VDIM : VDIM + 1]
                att[:, at] = shared_out.T.astype(jnp.bfloat16)
            else:
                top[h] = jnp.broadcast_to(high, (8, ROWS))
                acc[h] = summed

    def landed_slot(slot):
        for made in arrivals[slot]:
            made.wait_recv()

    shared = {0: share(0)}

    def pass_on(*slots):
        for slot in slots:
            landed_slot(slot)
            shared[slot] = share(slot)

    for h in range(HEADS):
        loads["k", h].wait()
    shared[0].wait_recv()
    attend(0, True, False, lambda: pass_on(1, 3))
    shared[1].wait_recv()
    attend(1, False, False, lambda: pass_on(2))
    shared[3].wait_recv()
    attend(3, False, False, lambda: None)
    shared[2].wait_recv()
    attend(2, False, True, lambda: None)

    above, below, far = turn(z, 1), turn(z, 3), turn(z, 2)
    left, right = pl.ds(0, HALF), pl.ds(HALF, HALF)
    copies = {}

    def copy(src, dst, j, n, to):
        made = remote(src, dst, send.at[j, n], recv.at[j, n], to)
        made.start()
        sent.append(made)
        copies[j, n] = made

    def own_residual(j):
        return residual[:, columns[j]].astype(jnp.float32)

    def spread(j, side):
        copy(part.at[j, side, far, :, left], early.at[j, 0, side], j, 0, z_to[1])
        copy(part.at[j, side, far, :, right], early.at[j, 1, side], j, 1, z_to[3])
        copy(part.at[j, side, above, :, right], late.at[j, 0, side, :, right], j, 2, z_to[1])
        copy(part.at[j, side, below, :, left], late.at[j, 1, side, :, left], j, 3, z_to[3])

    def relay(j, side):
        copies[j, 0].wait_recv()
        mine = part.at[j, side, above, :, left]
        mine[...] = (wide(mine) + wide(early.at[j, 0, side])).astype(jnp.bfloat16)
        copy(mine, late.at[j, 0, side, :, left], j, 4, z_to[1])
        copies[j, 1].wait_recv()
        mine = part.at[j, side, below, :, right]
        mine[...] = (wide(mine) + wide(early.at[j, 1, side])).astype(jnp.bfloat16)
        copy(mine, late.at[j, 1, side, :, right], j, 5, z_to[3])

    def landed(j):
        for n in (2, 3, 4, 5):
            copies[j, n].wait_recv()

    def ring_sum(j, side):
        return wide(part.at[j, side, z]) + wide(late.at[j, 0, side]) + wide(late.at[j, 1, side])

    def finish(j, value):
        final[j] = value.astype(jnp.bfloat16)
        copy(final.at[j], out.at[0, :, columns[j]], j, 7, pp_to)

    def product(j):
        loads["w", j].wait()
        made = jnp.dot(att[...], wv[j], preferred_element_type=jnp.float32)
        part[j] = made.astype(jnp.bfloat16).reshape(2, 4, LATROWS, PIECE)

    def z_step(j, step):
        if step == 0:
            product(j)
            spread(j, slice(None))
        elif step == 1:
            relay(j, slice(None))
        elif step == 2:
            landed(j)
            part[j, a, z] = (ring_sum(j, a) + own_residual(j)).astype(jnp.bfloat16)
            copy(part.at[j, a, z], crossed.at[j, 0], j, 6, x_to)
        elif step == 3:
            copies[j, 6].wait_recv()
            finish(j, ring_sum(j, 1 - a) + wide(crossed.at[j, 0]))

    def x_step(j, step):
        if step == 0:
            product(j)
            part[j, a, z] = (wide(part.at[j, a, z]) + own_residual(j)).astype(jnp.bfloat16)
            copy(part.at[j, a], crossed.at[j], j, 6, x_to)
        elif step == 1:
            copies[j, 6].wait_recv()
            part[j, 1 - a] = (wide(part.at[j, 1 - a]) + wide(crossed.at[j])).astype(jnp.bfloat16)
            spread(j, 1 - a)
        elif step == 2:
            relay(j, 1 - a)
        elif step == 3:
            landed(j)
            finish(j, ring_sum(j, 1 - a))

    steps = {"z": z_step, "x": x_step}
    loads["residual"].wait()
    for j, kind in enumerate(PIECES):
        steps[kind](j, 0)
    for j, step in ORDER:
        steps[PIECES[j]](j, step)
    for j in range(len(PIECES)):
        copies[j, 7].wait_recv()
    for made in sent:
        made.wait_send()


def local(queries, latents, latent_gain, w_ukv, w_o, residual, block_order):
    n = len(PIECES)
    hbm = pl.BlockSpec(memory_space=pltpu.HBM)
    bf16, f32 = jnp.bfloat16, jnp.float32
    dma = pltpu.SemaphoreType.DMA
    return pl.pallas_call(
        layer_kernel,
        out_shape=jax.ShapeDtypeStruct((1, LATROWS, D), bf16),
        in_specs=[hbm] * 8,
        out_specs=pl.BlockSpec(memory_space=pltpu.VMEM),
        scratch_shapes=[
            pltpu.VMEM((LATROWS, LATENT + ROPE), bf16),
            pltpu.VMEM((1, LATENT), f32),
            pltpu.VMEM((2, BLOCK + 16, 128), f32),
            pltpu.SMEM((1, 16), jnp.int32),
            pltpu.VMEM((ROWS, HEADS * (NOPE + ROPE)), bf16),
            pltpu.VMEM((LATENT, HEADS * NOPE), bf16),
            pltpu.VMEM((LATENT, HEADS * VDIM), bf16),
            pltpu.VMEM((n, HEADS * VDIM, PIECE), bf16),
            pltpu.VMEM((LATROWS, D), bf16),
            pltpu.VMEM((4, 2, 2, 2, 4, 16, KW), bf16),
            pltpu.VMEM((HEADS, 256, ROWS), bf16),
            pltpu.VMEM((HEADS * VDIM, LATENT), bf16),
            pltpu.VMEM((CHUNK, HEADS * NOPE), bf16),
            pltpu.VMEM((HEADS * VDIM, CHUNK), bf16),
            pltpu.VMEM((CHUNK, ROWS), f32),
            pltpu.VMEM((HEADS, 8, ROWS), f32),
            pltpu.VMEM((HEADS, VDIM + 16, ROWS), f32),
            pltpu.VMEM((ROWS, HEADS * VDIM), bf16),
            pltpu.VMEM((n, 2, 4, LATROWS, PIECE), bf16),
            pltpu.VMEM((n, 2, 2, LATROWS, HALF), bf16),
            pltpu.VMEM((n, 2, 2, LATROWS, PIECE), bf16),
            pltpu.VMEM((n, 4, LATROWS, PIECE), bf16),
            pltpu.VMEM((n, LATROWS, PIECE), bf16),
            dma((6,)),
            dma((2 * HEADS,)),
            dma((n,)),
            dma((17,)),
            dma((17,)),
            dma((n, 8)),
            dma((n, 8)),
        ],
        compiler_params=pltpu.CompilerParams(
            collective_id=0, has_side_effects=True, vmem_limit_bytes=58 * 2**20
        ),
        name="layer",
    )(latents, latent_gain, jnp.asarray(rope_tables()), block_order, queries, w_ukv, w_o, residual)


def solution(mesh):
    in_specs = (
        P("pp", "ctx", "tp"),
        P("pp", ("ctx", "tp"), None),
        P("pp", None),
        P("pp", None, "tp"),
        P("pp", "tp", None),
        P("pp", ("ctx", "tp"), None),
        P("pp", None),
    )
    out_specs = P("pp", ("ctx", "tp"), None)
    return jax.shard_map(local, mesh=mesh, in_specs=in_specs, out_specs=out_specs, check_vma=False)
```

```python
import math

import jax
import jax.numpy as jnp
import numpy as np
from jax import lax
from jax.experimental import pallas as pl
from jax.experimental.pallas import tpu as pltpu
from jax.sharding import PartitionSpec as P

NOPE = 128
ROPE = 64
VDIM = 128
LATENT = 512
BLOCK = 128
HEADS = 8
ROWS = 256
LATROWS = 32
D = 7168
KW = LATENT + 128
CHUNK = 512
PIECE = 1024
HALF = PIECE // 2
PIECES = ("x", "z", "x", "z", "x", "z", "z")
ORDER = (
    (1, 1), (3, 1), (0, 1), (5, 1), (6, 1), (2, 1), (1, 2), (3, 2), (0, 2), (4, 1), (5, 2),
    (1, 3), (6, 2), (3, 3), (2, 2), (0, 3), (5, 3), (4, 2), (6, 3), (2, 3), (4, 3),
)
SCALE2 = 0.135 * math.log2(math.e)

MESH = pl.DeviceIdType.MESH


def device(y, k, a, z, p):
    return (y * 2 + k, a * 4 + z, p)


def turn(v, n):
    return lax.rem(v + n, 4)


def rope_tables():
    f = 10000.0 ** (-(np.arange(32, dtype=np.float64) * 2.0 / ROPE))
    lane_f = np.tile(f, 4)
    sign = np.tile(np.concatenate([-np.ones(32), np.ones(32)]), 2)
    inner = np.arange(BLOCK, dtype=np.float64)[:, None] * lane_f
    outer = np.arange(16, dtype=np.float64)[:, None] * BLOCK * lane_f
    within = np.stack([np.cos(inner), np.sin(inner) * sign]).astype(np.float32)
    blocks = np.stack([np.cos(outer), np.sin(outer) * sign]).astype(np.float32)
    return np.concatenate([within, blocks], axis=1)


def rotation(tables, which, first, count):
    c_in = tables[0, pl.ds(first, count), :]
    s_in = tables[1, pl.ds(first, count), :]
    c_out = tables[0, pl.ds(BLOCK + which, 1), :]
    s_out = tables[1, pl.ds(BLOCK + which, 1), :]
    return c_out * c_in - s_out * s_in, s_out * c_in + c_out * s_in


def swapped(v):
    return jnp.concatenate([v[:, 32:64], v[:, :32], v[:, 96:], v[:, 64:96]], axis=1)


def remote(src, dst, send, recv, to):
    return pltpu.make_async_remote_copy(
        src_ref=src, dst_ref=dst, send_sem=send, recv_sem=recv, device_id=to, device_id_type=MESH
    )


def wide(ref):
    return ref[...].astype(jnp.float32)


def layer_kernel(
    lat_in, gain_in, tables_in, order_in, q_in, up_in, w_in, residual_in,
    out,
    lat, gain, tables, order, q, up_k, up_v, wv, residual,
    kl, q_t, up_vt, key, value_t, bias, top, acc, att,
    part, early, late, crossed, final,
    load_sem, up_sem, w_sem, g_send, g_recv, send, recv,
):
    c = lax.axis_index("ctx")
    t = lax.axis_index("tp")
    p = lax.axis_index("pp")
    y, k, a, z = c // 2, lax.rem(c, 2), t // 4, lax.rem(t, 4)
    z_to = {n: device(y, k, a, turn(z, n), p) for n in (1, 3, 2)}
    y_to = {n: device(turn(y, n), k, a, z, p) for n in (1, 3, 2)}
    x_to = device(y, k, 1 - a, z, p)
    k_to = device(y, 1 - k, a, z, p)
    pp_to = device(y, k, 1 - a, z, 1 - p)

    loads = {}

    def load(name, src, dst, sem):
        made = pltpu.make_async_copy(src, dst, sem)
        made.start()
        loads[name] = made

    load("lat", lat_in.at[0], lat, load_sem.at[0])
    load("order", order_in, order, load_sem.at[1])
    load("gain", gain_in, gain, load_sem.at[2])
    load("tables", tables_in, tables, load_sem.at[3])
    barrier = pltpu.get_barrier_semaphore()
    for to in [*z_to.values(), *y_to.values(), x_to, k_to, pp_to]:
        pl.semaphore_signal(barrier, inc=1, device_id=to, device_id_type=MESH)

    load("q", q_in.at[0], q, load_sem.at[4])
    for h in range(HEADS):
        at = pl.ds(h * VDIM, VDIM)
        load(("k", h), up_in.at[0, :, pl.ds(h * 256, NOPE)], up_k.at[:, at], up_sem.at[h])
        load(("v", h), up_in.at[0, :, pl.ds(h * 256 + NOPE, VDIM)], up_v.at[:, at], up_sem.at[8 + h])
    columns = [pl.ds(j * PIECE, PIECE) for j in range(len(PIECES))]

    for name in ("lat", "order", "gain", "tables"):
        loads[name].wait()
    rows = lat[...].astype(jnp.float32)
    low_rank = rows[:, :LATENT]
    scale = lax.rsqrt(jnp.mean(low_rank * low_rank, axis=-1, keepdims=True) + 1e-6)
    normed = (low_rank * scale * gain[...]).astype(jnp.bfloat16)
    twice = jnp.concatenate([rows[:, LATENT:], rows[:, LATENT:]], axis=1)
    cos, sin = rotation(tables, order[0, c * 2 + a], z * LATROWS, LATROWS)
    roped = ((twice * cos + swapped(twice) * sin) * SCALE2).astype(jnp.bfloat16)
    own = jnp.concatenate([normed, roped], axis=1)
    kl[0, 0, 0, 0, 0] = own[:16]
    kl[0, 1, 0, 0, 0] = own[16:]
    pl.semaphore_wait(barrier, 9)

    sent = []

    def push(src, dst, n, to):
        made = remote(src, dst, g_send.at[n], g_recv.at[n], to)
        made.start()
        sent.append(made)
        return made

    to_x = push(kl.at[0, :, 0, 0, 0], kl.at[0, :, 0, 1, 0], 0, x_to)

    loads["q"].wait()
    lane = lax.broadcasted_iota(jnp.int32, (BLOCK, 128), 1)
    for half in range(2):
        cos, sin = rotation(tables, order[0, c * 2 + half], 0, BLOCK)
        at = pl.ds(half * BLOCK, BLOCK)
        for pair in range(HEADS // 2):
            both = q[at, pair * 384 : (pair + 1) * 384].astype(jnp.float32)
            v = jnp.concatenate([both[:, 128:192], both[:, 320:384]], axis=1)
            turned = v * cos + swapped(v) * sin
            q_t[pair * 2, :NOPE, at] = both[:, :128].T.astype(jnp.bfloat16)
            q_t[pair * 2, NOPE:, at] = jnp.where(lane < ROPE, turned, 0.0).T.astype(jnp.bfloat16)
            q_t[pair * 2 + 1, :NOPE, at] = both[:, 192:320].T.astype(jnp.bfloat16)
            q_t[pair * 2 + 1, NOPE:, at] = jnp.where(lane < ROPE, 0.0, turned).T.astype(jnp.bfloat16)

    to_x.wait_recv()
    near = []
    for i, n in enumerate((1, 3, 2)):
        near.append(push(kl.at[0, 0, 0, :, 0], kl.at[0, 0, 0, :, 4 - n], 1 + i, z_to[n]))
        near.append(push(kl.at[0, 1, 0, :, 0], kl.at[0, 1, 0, :, 4 - n], 4 + i, y_to[n]))
    for h in range(HEADS):
        loads["v", h].wait()
        at = pl.ds(h * VDIM, VDIM)
        up_vt[at, :] = up_v[:, at].astype(jnp.float32).T.astype(jnp.bfloat16)
    for made in near:
        made.wait_recv()
    arrivals = {}
    for i, n in enumerate((3, 1)):
        arrivals[4 - n] = (
            push(kl.at[0, 0, 0], kl.at[4 - n, 0, 0], 7 + i, y_to[n]),
            push(kl.at[0, 1, 0], kl.at[4 - n, 1, 0], 9 + i, z_to[n]),
        )

    def forward(slot):
        side, to = (0, 3) if slot == 1 else (1, 1)
        return (
            push(kl.at[slot, 0, 0, side], kl.at[2, 0, 0, side], 11 + side, y_to[to]),
            push(kl.at[slot, 1, 0, side], kl.at[2, 1, 0, side], 17 + side, z_to[to]),
        )

    def share(slot):
        return push(kl.at[slot, :, 0], kl.at[slot, :, 1], 13 + slot, k_to)

    row = lax.broadcasted_iota(jnp.int32, (BLOCK, BLOCK), 0)
    second = row >= 64
    minor = lax.rem(row, 64) // 16
    deep = lax.rem(row, 16)
    query_in = lax.broadcasted_iota(jnp.int32, (BLOCK, BLOCK), 1)
    query_at = [order[0, c * 2 + n] * BLOCK + query_in for n in range(2)]

    def mask(slot):
        for half in range(2):
            for core in range(2):
                here = k if core == 0 else 1 - k
                if half == 0:
                    there = (turn(y, slot) * 2 + here) * 2
                    block = jnp.where(second, order[0, there + 1 - a], order[0, there + a])
                    key_at = block * BLOCK + lax.rem(minor + z, 4) * LATROWS + deep
                else:
                    block = jnp.zeros_like(row)
                    for m in range(4):
                        there = (turn(y, m) * 2 + here) * 2
                        one = jnp.where(second, order[0, there + 1 - a], order[0, there + a])
                        block = jnp.where(minor == m, one, block)
                    key_at = block * BLOCK + turn(z, slot) * LATROWS + 16 + deep
                for n in range(2):
                    bias[pl.ds((half * 2 + core) * BLOCK, BLOCK), pl.ds(n * BLOCK, BLOCK)] = jnp.where(
                        key_at <= query_at[n], 0.0, -1e30
                    )

    ones = jnp.ones((16, CHUNK), jnp.bfloat16)

    def attend(slot, first, last, between):
        mask(slot)
        latent = kl[slot].reshape(CHUNK, KW)
        low_rank, key_rope = latent[:, :LATENT], latent[:, LATENT:]
        for n in range(4):
            at = pl.ds(n * 256, 256)
            made = jnp.dot(low_rank, up_k[:, at], preferred_element_type=jnp.float32)
            key[:, at] = (made * SCALE2).astype(jnp.bfloat16)
        for n in range(4):
            at = pl.ds(n * 256, 256)
            value_t[at, :] = lax.dot_general(
                up_vt[at, :], low_rank, (((1,), (1,)), ((), ())), preferred_element_type=jnp.float32
            ).astype(jnp.bfloat16)
        for h in range(HEADS):
            if h == 5:
                between()
            at = pl.ds(h * VDIM, VDIM)
            keys = jnp.concatenate([key[:, at], key_rope], axis=1)
            scores = jnp.dot(keys, q_t[h], preferred_element_type=jnp.float32) + bias[...]
            high = jnp.max(scores, axis=0, keepdims=True)
            if not first:
                before = top[h, :1]
                high = jnp.maximum(before, high)
            weights = jnp.exp2(scores - high).astype(jnp.bfloat16)
            values = jnp.concatenate([value_t[at, :], ones], axis=0)
            summed = jnp.dot(values, weights, preferred_element_type=jnp.float32)
            if not first:
                summed = summed + acc[h] * jnp.exp2(before - high)
            if last:
                shared_out = summed[:VDIM] / summed[VDIM : VDIM + 1]
                att[:, at] = shared_out.T.astype(jnp.bfloat16)
            else:
                top[h] = jnp.broadcast_to(high, (8, ROWS))
                acc[h] = summed

    def landed_slot(slot):
        for made in arrivals[slot]:
            made.wait_recv()

    shared = {0: share(0)}

    def pass_on(*slots):
        if slots == (1, 3):
            landed_slot(1)
            ahead = forward(1)
            landed_slot(3)
            arrivals[2] = ahead + forward(3)
        else:
            landed_slot(2)
        for slot in slots:
            shared[slot] = share(slot)

    for h in range(HEADS):
        loads["k", h].wait()
    shared[0].wait_recv()
    load("residual", residual_in.at[0], residual, load_sem.at[5])
    for j in range(len(PIECES)):
        load(("w", j), w_in.at[0, :, columns[j]], wv.at[j], w_sem.at[j])
    attend(0, True, False, lambda: pass_on(1, 3))
    shared[1].wait_recv()
    attend(1, False, False, lambda: pass_on(2))
    shared[3].wait_recv()
    attend(3, False, False, lambda: None)
    shared[2].wait_recv()
    attend(2, False, True, lambda: None)

    above, below, far = turn(z, 1), turn(z, 3), turn(z, 2)
    left, right = pl.ds(0, HALF), pl.ds(HALF, HALF)
    copies = {}

    def copy(src, dst, j, n, to):
        made = remote(src, dst, send.at[j, n], recv.at[j, n], to)
        made.start()
        sent.append(made)
        copies[j, n] = made

    def own_residual(j):
        return residual[:, columns[j]].astype(jnp.float32)

    def spread(j, side):
        copy(part.at[j, side, far, :, left], early.at[j, 0, side], j, 0, z_to[1])
        copy(part.at[j, side, far, :, right], early.at[j, 1, side], j, 1, z_to[3])
        copy(part.at[j, side, above, :, right], late.at[j, 0, side, :, right], j, 2, z_to[1])
        copy(part.at[j, side, below, :, left], late.at[j, 1, side, :, left], j, 3, z_to[3])

    def relay(j, side):
        copies[j, 0].wait_recv()
        mine = part.at[j, side, above, :, left]
        mine[...] = (wide(mine) + wide(early.at[j, 0, side])).astype(jnp.bfloat16)
        copy(mine, late.at[j, 0, side, :, left], j, 4, z_to[1])
        copies[j, 1].wait_recv()
        mine = part.at[j, side, below, :, right]
        mine[...] = (wide(mine) + wide(early.at[j, 1, side])).astype(jnp.bfloat16)
        copy(mine, late.at[j, 1, side, :, right], j, 5, z_to[3])

    def landed(j):
        for n in (2, 3, 4, 5):
            copies[j, n].wait_recv()

    def ring_sum(j, side):
        return wide(part.at[j, side, z]) + wide(late.at[j, 0, side]) + wide(late.at[j, 1, side])

    def finish(j, value):
        final[j] = value.astype(jnp.bfloat16)
        copy(final.at[j], out.at[0, :, columns[j]], j, 7, pp_to)

    def product(j):
        loads["w", j].wait()
        made = jnp.dot(att[...], wv[j], preferred_element_type=jnp.float32)
        part[j] = made.astype(jnp.bfloat16).reshape(2, 4, LATROWS, PIECE)

    def z_step(j, step):
        if step == 0:
            product(j)
            spread(j, slice(None))
        elif step == 1:
            relay(j, slice(None))
        elif step == 2:
            landed(j)
            part[j, a, z] = (ring_sum(j, a) + own_residual(j)).astype(jnp.bfloat16)
            copy(part.at[j, a, z], crossed.at[j, 0], j, 6, x_to)
        elif step == 3:
            copies[j, 6].wait_recv()
            finish(j, ring_sum(j, 1 - a) + wide(crossed.at[j, 0]))

    def x_step(j, step):
        if step == 0:
            product(j)
            part[j, a, z] = (wide(part.at[j, a, z]) + own_residual(j)).astype(jnp.bfloat16)
            copy(part.at[j, a], crossed.at[j], j, 6, x_to)
        elif step == 1:
            copies[j, 6].wait_recv()
            part[j, 1 - a] = (wide(part.at[j, 1 - a]) + wide(crossed.at[j])).astype(jnp.bfloat16)
            spread(j, 1 - a)
        elif step == 2:
            relay(j, 1 - a)
        elif step == 3:
            landed(j)
            finish(j, ring_sum(j, 1 - a))

    steps = {"z": z_step, "x": x_step}
    loads["residual"].wait()
    for j, kind in enumerate(PIECES):
        steps[kind](j, 0)
    for j, step in ORDER:
        steps[PIECES[j]](j, step)
    for j in range(len(PIECES)):
        copies[j, 7].wait_recv()
    for made in sent:
        made.wait_send()


def local(queries, latents, latent_gain, w_ukv, w_o, residual, block_order):
    n = len(PIECES)
    hbm = pl.BlockSpec(memory_space=pltpu.HBM)
    bf16, f32 = jnp.bfloat16, jnp.float32
    dma = pltpu.SemaphoreType.DMA
    return pl.pallas_call(
        layer_kernel,
        out_shape=jax.ShapeDtypeStruct((1, LATROWS, D), bf16),
        in_specs=[hbm] * 8,
        out_specs=pl.BlockSpec(memory_space=pltpu.VMEM),
        scratch_shapes=[
            pltpu.VMEM((LATROWS, LATENT + ROPE), bf16),
            pltpu.VMEM((1, LATENT), f32),
            pltpu.VMEM((2, BLOCK + 16, 128), f32),
            pltpu.SMEM((1, 16), jnp.int32),
            pltpu.VMEM((ROWS, HEADS * (NOPE + ROPE)), bf16),
            pltpu.VMEM((LATENT, HEADS * NOPE), bf16),
            pltpu.VMEM((LATENT, HEADS * VDIM), bf16),
            pltpu.VMEM((n, HEADS * VDIM, PIECE), bf16),
            pltpu.VMEM((LATROWS, D), bf16),
            pltpu.VMEM((4, 2, 2, 2, 4, 16, KW), bf16),
            pltpu.VMEM((HEADS, 256, ROWS), bf16),
            pltpu.VMEM((HEADS * VDIM, LATENT), bf16),
            pltpu.VMEM((CHUNK, HEADS * NOPE), bf16),
            pltpu.VMEM((HEADS * VDIM, CHUNK), bf16),
            pltpu.VMEM((CHUNK, ROWS), f32),
            pltpu.VMEM((HEADS, 8, ROWS), f32),
            pltpu.VMEM((HEADS, VDIM + 16, ROWS), f32),
            pltpu.VMEM((ROWS, HEADS * VDIM), bf16),
            pltpu.VMEM((n, 2, 4, LATROWS, PIECE), bf16),
            pltpu.VMEM((n, 2, 2, LATROWS, HALF), bf16),
            pltpu.VMEM((n, 2, 2, LATROWS, PIECE), bf16),
            pltpu.VMEM((n, 4, LATROWS, PIECE), bf16),
            pltpu.VMEM((n, LATROWS, PIECE), bf16),
            dma((6,)),
            dma((2 * HEADS,)),
            dma((n,)),
            dma((19,)),
            dma((19,)),
            dma((n, 8)),
            dma((n, 8)),
        ],
        compiler_params=pltpu.CompilerParams(
            collective_id=0, has_side_effects=True, vmem_limit_bytes=58 * 2**20
        ),
        name="layer",
    )(latents, latent_gain, jnp.asarray(rope_tables()), block_order, queries, w_ukv, w_o, residual)


def solution(mesh):
    in_specs = (
        P("pp", "ctx", "tp"),
        P("pp", ("ctx", "tp"), None),
        P("pp", None),
        P("pp", None, "tp"),
        P("pp", "tp", None),
        P("pp", ("ctx", "tp"), None),
        P("pp", None),
    )
    out_specs = P("pp", ("ctx", "tp"), None)
    return jax.shard_map(local, mesh=mesh, in_specs=in_specs, out_specs=out_specs, check_vma=False)
```

```python
import math

import jax
import jax.numpy as jnp
import numpy as np
from jax import lax
from jax.experimental import pallas as pl
from jax.experimental.pallas import tpu as pltpu
from jax.sharding import PartitionSpec as P

NOPE = 128
ROPE = 64
VDIM = 128
LATENT = 512
BLOCK = 128
HEADS = 8
ROWS = 256
LATROWS = 32
D = 7168
KW = LATENT + 128
CHUNK = 512
PIECE = 1024
HALF = PIECE // 2
PIECES = ("x", "z", "x", "z", "x", "z", "z")
ORDER = (
    (1, 1), (3, 1), (0, 1), (5, 1), (6, 1), (2, 1), (1, 2), (3, 2), (0, 2), (4, 1), (5, 2),
    (1, 3), (6, 2), (3, 3), (2, 2), (0, 3), (5, 3), (4, 2), (6, 3), (2, 3), (4, 3),
)
SCALE2 = 0.135 * math.log2(math.e)

MESH = pl.DeviceIdType.MESH


def device(y, k, a, z, p):
    return (y * 2 + k, a * 4 + z, p)


def turn(v, n):
    return lax.rem(v + n, 4)


def rope_tables():
    f = 10000.0 ** (-(np.arange(32, dtype=np.float64) * 2.0 / ROPE))
    lane_f = np.tile(f, 4)
    sign = np.tile(np.concatenate([-np.ones(32), np.ones(32)]), 2)
    inner = np.arange(BLOCK, dtype=np.float64)[:, None] * lane_f
    outer = np.arange(16, dtype=np.float64)[:, None] * BLOCK * lane_f
    within = np.stack([np.cos(inner), np.sin(inner) * sign]).astype(np.float32)
    blocks = np.stack([np.cos(outer), np.sin(outer) * sign]).astype(np.float32)
    return np.concatenate([within, blocks], axis=1)


def rotation(tables, which, first, count):
    c_in = tables[0, pl.ds(first, count), :]
    s_in = tables[1, pl.ds(first, count), :]
    c_out = tables[0, pl.ds(BLOCK + which, 1), :]
    s_out = tables[1, pl.ds(BLOCK + which, 1), :]
    return c_out * c_in - s_out * s_in, s_out * c_in + c_out * s_in


def swapped(v):
    return jnp.concatenate([v[:, 32:64], v[:, :32], v[:, 96:], v[:, 64:96]], axis=1)


def remote(src, dst, send, recv, to):
    return pltpu.make_async_remote_copy(
        src_ref=src, dst_ref=dst, send_sem=send, recv_sem=recv, device_id=to, device_id_type=MESH
    )


def wide(ref):
    return ref[...].astype(jnp.float32)


def layer_kernel(
    lat_in, gain_in, tables_in, order_in, q_in, up_in, w_in, residual_in,
    out,
    lat, gain, tables, order, q, up_k, up_v, wv, residual,
    kl, q_t, up_vt, key, value_t, bias, top, acc, att,
    part, early, late, crossed, final,
    load_sem, up_sem, w_sem, g_send, g_recv, send, recv,
):
    c = lax.axis_index("ctx")
    t = lax.axis_index("tp")
    p = lax.axis_index("pp")
    y, k, a, z = c // 2, lax.rem(c, 2), t // 4, lax.rem(t, 4)
    z_to = {n: device(y, k, a, turn(z, n), p) for n in (1, 3, 2)}
    y_to = {n: device(turn(y, n), k, a, z, p) for n in (1, 3, 2)}
    x_to = device(y, k, 1 - a, z, p)
    k_to = device(y, 1 - k, a, z, p)
    pp_to = device(y, k, 1 - a, z, 1 - p)

    loads = {}

    def load(name, src, dst, sem):
        made = pltpu.make_async_copy(src, dst, sem)
        made.start()
        loads[name] = made

    load("lat", lat_in.at[0], lat, load_sem.at[0])
    load("order", order_in, order, load_sem.at[1])
    load("gain", gain_in, gain, load_sem.at[2])
    load("tables", tables_in, tables, load_sem.at[3])
    barrier = pltpu.get_barrier_semaphore()
    for to in [*z_to.values(), *y_to.values(), x_to, k_to, pp_to]:
        pl.semaphore_signal(barrier, inc=1, device_id=to, device_id_type=MESH)

    load("q", q_in.at[0], q, load_sem.at[4])
    for h in range(HEADS):
        at = pl.ds(h * VDIM, VDIM)
        load(("k", h), up_in.at[0, :, pl.ds(h * 256, NOPE)], up_k.at[:, at], up_sem.at[h])
        load(("v", h), up_in.at[0, :, pl.ds(h * 256 + NOPE, VDIM)], up_v.at[:, at], up_sem.at[8 + h])
    columns = [pl.ds(j * PIECE, PIECE) for j in range(len(PIECES))]

    for name in ("lat", "order", "gain", "tables"):
        loads[name].wait()
    rows = lat[...].astype(jnp.float32)
    low_rank = rows[:, :LATENT]
    scale = lax.rsqrt(jnp.mean(low_rank * low_rank, axis=-1, keepdims=True) + 1e-6)
    normed = (low_rank * scale * gain[...]).astype(jnp.bfloat16)
    twice = jnp.concatenate([rows[:, LATENT:], rows[:, LATENT:]], axis=1)
    cos, sin = rotation(tables, order[0, c * 2 + a], z * LATROWS, LATROWS)
    roped = ((twice * cos + swapped(twice) * sin) * SCALE2).astype(jnp.bfloat16)
    own = jnp.concatenate([normed, roped], axis=1)
    kl[0, 0, 0, 0, 0] = own[:16]
    kl[0, 1, 0, 0, 0] = own[16:]
    pl.semaphore_wait(barrier, 9)

    sent = []

    def push(src, dst, n, to):
        made = remote(src, dst, g_send.at[n], g_recv.at[n], to)
        made.start()
        sent.append(made)
        return made

    to_x = push(kl.at[0, :, 0, 0, 0], kl.at[0, :, 0, 1, 0], 0, x_to)

    loads["q"].wait()
    lane = lax.broadcasted_iota(jnp.int32, (BLOCK, 128), 1)
    for half in range(2):
        cos, sin = rotation(tables, order[0, c * 2 + half], 0, BLOCK)
        at = pl.ds(half * BLOCK, BLOCK)
        for pair in range(HEADS // 2):
            both = q[at, pair * 384 : (pair + 1) * 384].astype(jnp.float32)
            v = jnp.concatenate([both[:, 128:192], both[:, 320:384]], axis=1)
            turned = v * cos + swapped(v) * sin
            q_t[pair * 2, :NOPE, at] = both[:, :128].T.astype(jnp.bfloat16)
            q_t[pair * 2, NOPE:, at] = jnp.where(lane < ROPE, turned, 0.0).T.astype(jnp.bfloat16)
            q_t[pair * 2 + 1, :NOPE, at] = both[:, 192:320].T.astype(jnp.bfloat16)
            q_t[pair * 2 + 1, NOPE:, at] = jnp.where(lane < ROPE, 0.0, turned).T.astype(jnp.bfloat16)

    to_x.wait_recv()
    near = []
    for i, n in enumerate((1, 3, 2)):
        near.append(push(kl.at[0, 0, 0, :, 0], kl.at[0, 0, 0, :, 4 - n], 1 + i, z_to[n]))
        near.append(push(kl.at[0, 1, 0, :, 0], kl.at[0, 1, 0, :, 4 - n], 4 + i, y_to[n]))
    for h in range(HEADS):
        loads["v", h].wait()
        at = pl.ds(h * VDIM, VDIM)
        up_vt[at, :] = up_v[:, at].astype(jnp.float32).T.astype(jnp.bfloat16)
    for made in near:
        made.wait_recv()
    arrivals = {}
    for i, n in enumerate((3, 1)):
        arrivals[4 - n] = (
            push(kl.at[0, 0, 0], kl.at[4 - n, 0, 0], 7 + i, y_to[n]),
            push(kl.at[0, 1, 0], kl.at[4 - n, 1, 0], 9 + i, z_to[n]),
        )

    def forward(slot):
        side, to = (0, 3) if slot == 1 else (1, 1)
        return (
            push(kl.at[slot, 0, 0, side], kl.at[2, 0, 0, side], 11 + side, y_to[to]),
            push(kl.at[slot, 1, 0, side], kl.at[2, 1, 0, side], 17 + side, z_to[to]),
        )

    def share(slot):
        return push(kl.at[slot, :, 0], kl.at[slot, :, 1], 13 + slot, k_to)

    row = lax.broadcasted_iota(jnp.int32, (BLOCK, BLOCK), 0)
    second = row >= 64
    minor = lax.rem(row, 64) // 16
    deep = lax.rem(row, 16)
    query_in = lax.broadcasted_iota(jnp.int32, (BLOCK, BLOCK), 1)
    query_at = [order[0, c * 2 + n] * BLOCK + query_in for n in range(2)]

    def mask(slot):
        for half in range(2):
            for core in range(2):
                here = k if core == 0 else 1 - k
                if half == 0:
                    there = (turn(y, slot) * 2 + here) * 2
                    block = jnp.where(second, order[0, there + 1 - a], order[0, there + a])
                    key_at = block * BLOCK + lax.rem(minor + z, 4) * LATROWS + deep
                else:
                    block = jnp.zeros_like(row)
                    for m in range(4):
                        there = (turn(y, m) * 2 + here) * 2
                        one = jnp.where(second, order[0, there + 1 - a], order[0, there + a])
                        block = jnp.where(minor == m, one, block)
                    key_at = block * BLOCK + turn(z, slot) * LATROWS + 16 + deep
                for n in range(2):
                    bias[pl.ds((half * 2 + core) * BLOCK, BLOCK), pl.ds(n * BLOCK, BLOCK)] = jnp.where(
                        key_at <= query_at[n], 0.0, -1e30
                    )

    ones = jnp.ones((16, CHUNK), jnp.bfloat16)

    def attend(slot, first, last, between):
        latent = kl[slot].reshape(CHUNK, KW)
        low_rank, key_rope = latent[:, :LATENT], latent[:, LATENT:]

        def make_keys(n):
            at = pl.ds(n * 256, 256)
            made = jnp.dot(low_rank, up_k[:, at], preferred_element_type=jnp.float32)
            key[:, at] = (made * SCALE2).astype(jnp.bfloat16)

        def make_values(n):
            at = pl.ds(n * 256, 256)
            value_t[at, :] = lax.dot_general(
                up_vt[at, :], low_rank, (((1,), (1,)), ((), ())), preferred_element_type=jnp.float32
            ).astype(jnp.bfloat16)

        def score(h):
            keys = jnp.concatenate([key[:, pl.ds(h * VDIM, VDIM)], key_rope], axis=1)
            return jnp.dot(keys, q_t[h], preferred_element_type=jnp.float32) + bias[...]

        def soften(h, scores):
            high = jnp.max(scores, axis=0, keepdims=True)
            shrink = None
            if not first:
                before = top[h, :1]
                high = jnp.maximum(before, high)
                shrink = jnp.exp2(before - high)
            if not last:
                top[h] = jnp.broadcast_to(high, (8, ROWS))
            return jnp.exp2(scores - high).astype(jnp.bfloat16), shrink

        def gather_values(h, weights, shrink):
            at = pl.ds(h * VDIM, VDIM)
            values = jnp.concatenate([value_t[at, :], ones], axis=0)
            summed = jnp.dot(values, weights, preferred_element_type=jnp.float32)
            if not first:
                summed = summed + acc[h] * shrink
            if last:
                att[:, at] = (summed[:VDIM] / summed[VDIM : VDIM + 1]).T.astype(jnp.bfloat16)
            else:
                acc[h] = summed

        make_keys(0)
        mask(slot)
        make_values(0)
        scores, waiting = score(0), None
        for h in range(HEADS):
            if h == 5:
                between()
            more = h % 2 == 0 and h < 6
            if more:
                make_keys(h // 2 + 1)
            following = score(h + 1) if h < HEADS - 1 else None
            weights, shrink = soften(h, scores)
            if more:
                make_values(h // 2 + 1)
            if waiting:
                gather_values(*waiting)
            waiting, scores = (h, weights, shrink), following
        gather_values(*waiting)

    def landed_slot(slot):
        for made in arrivals[slot]:
            made.wait_recv()

    shared = {0: share(0)}

    def pass_on(*slots):
        if slots == (1, 3):
            landed_slot(1)
            ahead = forward(1)
            landed_slot(3)
            arrivals[2] = ahead + forward(3)
        else:
            landed_slot(2)
        for slot in slots:
            shared[slot] = share(slot)

    for h in range(HEADS):
        loads["k", h].wait()
    shared[0].wait_recv()
    load("residual", residual_in.at[0], residual, load_sem.at[5])
    for j in range(len(PIECES)):
        load(("w", j), w_in.at[0, :, columns[j]], wv.at[j], w_sem.at[j])
    attend(0, True, False, lambda: pass_on(1, 3))
    shared[1].wait_recv()
    attend(1, False, False, lambda: pass_on(2))
    shared[3].wait_recv()
    attend(3, False, False, lambda: None)
    shared[2].wait_recv()
    attend(2, False, True, lambda: None)

    above, below, far = turn(z, 1), turn(z, 3), turn(z, 2)
    left, right = pl.ds(0, HALF), pl.ds(HALF, HALF)
    copies = {}

    def copy(src, dst, j, n, to):
        made = remote(src, dst, send.at[j, n], recv.at[j, n], to)
        made.start()
        sent.append(made)
        copies[j, n] = made

    def own_residual(j):
        return residual[:, columns[j]].astype(jnp.float32)

    def spread(j, side):
        copy(part.at[j, side, far, :, left], early.at[j, 0, side], j, 0, z_to[1])
        copy(part.at[j, side, far, :, right], early.at[j, 1, side], j, 1, z_to[3])
        copy(part.at[j, side, above, :, right], late.at[j, 0, side, :, right], j, 2, z_to[1])
        copy(part.at[j, side, below, :, left], late.at[j, 1, side, :, left], j, 3, z_to[3])

    def relay(j, side):
        copies[j, 0].wait_recv()
        mine = part.at[j, side, above, :, left]
        mine[...] = (wide(mine) + wide(early.at[j, 0, side])).astype(jnp.bfloat16)
        copy(mine, late.at[j, 0, side, :, left], j, 4, z_to[1])
        copies[j, 1].wait_recv()
        mine = part.at[j, side, below, :, right]
        mine[...] = (wide(mine) + wide(early.at[j, 1, side])).astype(jnp.bfloat16)
        copy(mine, late.at[j, 1, side, :, right], j, 5, z_to[3])

    def landed(j):
        for n in (2, 3, 4, 5):
            copies[j, n].wait_recv()

    def ring_sum(j, side):
        return wide(part.at[j, side, z]) + wide(late.at[j, 0, side]) + wide(late.at[j, 1, side])

    def finish(j, value):
        final[j] = value.astype(jnp.bfloat16)
        copy(final.at[j], out.at[0, :, columns[j]], j, 7, pp_to)

    def product(j):
        loads["w", j].wait()
        made = jnp.dot(att[...], wv[j], preferred_element_type=jnp.float32)
        part[j] = made.astype(jnp.bfloat16).reshape(2, 4, LATROWS, PIECE)

    def z_step(j, step):
        if step == 0:
            product(j)
            spread(j, slice(None))
        elif step == 1:
            relay(j, slice(None))
        elif step == 2:
            landed(j)
            part[j, a, z] = (ring_sum(j, a) + own_residual(j)).astype(jnp.bfloat16)
            copy(part.at[j, a, z], crossed.at[j, 0], j, 6, x_to)
        elif step == 3:
            copies[j, 6].wait_recv()
            finish(j, ring_sum(j, 1 - a) + wide(crossed.at[j, 0]))

    def x_step(j, step):
        if step == 0:
            product(j)
            part[j, a, z] = (wide(part.at[j, a, z]) + own_residual(j)).astype(jnp.bfloat16)
            copy(part.at[j, a], crossed.at[j], j, 6, x_to)
        elif step == 1:
            copies[j, 6].wait_recv()
            part[j, 1 - a] = (wide(part.at[j, 1 - a]) + wide(crossed.at[j])).astype(jnp.bfloat16)
            spread(j, 1 - a)
        elif step == 2:
            relay(j, 1 - a)
        elif step == 3:
            landed(j)
            finish(j, ring_sum(j, 1 - a))

    steps = {"z": z_step, "x": x_step}
    loads["residual"].wait()
    for j, kind in enumerate(PIECES):
        steps[kind](j, 0)
    for j, step in ORDER:
        steps[PIECES[j]](j, step)
    for j in range(len(PIECES)):
        copies[j, 7].wait_recv()
    for made in sent:
        made.wait_send()


def local(queries, latents, latent_gain, w_ukv, w_o, residual, block_order):
    n = len(PIECES)
    hbm = pl.BlockSpec(memory_space=pltpu.HBM)
    bf16, f32 = jnp.bfloat16, jnp.float32
    dma = pltpu.SemaphoreType.DMA
    return pl.pallas_call(
        layer_kernel,
        out_shape=jax.ShapeDtypeStruct((1, LATROWS, D), bf16),
        in_specs=[hbm] * 8,
        out_specs=pl.BlockSpec(memory_space=pltpu.VMEM),
        scratch_shapes=[
            pltpu.VMEM((LATROWS, LATENT + ROPE), bf16),
            pltpu.VMEM((1, LATENT), f32),
            pltpu.VMEM((2, BLOCK + 16, 128), f32),
            pltpu.SMEM((1, 16), jnp.int32),
            pltpu.VMEM((ROWS, HEADS * (NOPE + ROPE)), bf16),
            pltpu.VMEM((LATENT, HEADS * NOPE), bf16),
            pltpu.VMEM((LATENT, HEADS * VDIM), bf16),
            pltpu.VMEM((n, HEADS * VDIM, PIECE), bf16),
            pltpu.VMEM((LATROWS, D), bf16),
            pltpu.VMEM((4, 2, 2, 2, 4, 16, KW), bf16),
            pltpu.VMEM((HEADS, 256, ROWS), bf16),
            pltpu.VMEM((HEADS * VDIM, LATENT), bf16),
            pltpu.VMEM((CHUNK, HEADS * NOPE), bf16),
            pltpu.VMEM((HEADS * VDIM, CHUNK), bf16),
            pltpu.VMEM((CHUNK, ROWS), f32),
            pltpu.VMEM((HEADS, 8, ROWS), f32),
            pltpu.VMEM((HEADS, VDIM + 16, ROWS), f32),
            pltpu.VMEM((ROWS, HEADS * VDIM), bf16),
            pltpu.VMEM((n, 2, 4, LATROWS, PIECE), bf16),
            pltpu.VMEM((n, 2, 2, LATROWS, HALF), bf16),
            pltpu.VMEM((n, 2, 2, LATROWS, PIECE), bf16),
            pltpu.VMEM((n, 4, LATROWS, PIECE), bf16),
            pltpu.VMEM((n, LATROWS, PIECE), bf16),
            dma((6,)),
            dma((2 * HEADS,)),
            dma((n,)),
            dma((19,)),
            dma((19,)),
            dma((n, 8)),
            dma((n, 8)),
        ],
        compiler_params=pltpu.CompilerParams(
            collective_id=0, has_side_effects=True, vmem_limit_bytes=58 * 2**20
        ),
        name="layer",
    )(latents, latent_gain, jnp.asarray(rope_tables()), block_order, queries, w_ukv, w_o, residual)


def solution(mesh):
    in_specs = (
        P("pp", "ctx", "tp"),
        P("pp", ("ctx", "tp"), None),
        P("pp", None),
        P("pp", None, "tp"),
        P("pp", "tp", None),
        P("pp", ("ctx", "tp"), None),
        P("pp", None),
    )
    out_specs = P("pp", ("ctx", "tp"), None)
    return jax.shard_map(local, mesh=mesh, in_specs=in_specs, out_specs=out_specs, check_vma=False)
```

```python
import math

import jax
import jax.numpy as jnp
import numpy as np
from jax import lax
from jax.experimental import pallas as pl
from jax.experimental.pallas import tpu as pltpu
from jax.sharding import PartitionSpec as P

NOPE = 128
ROPE = 64
VDIM = 128
LATENT = 512
BLOCK = 128
HEADS = 8
ROWS = 256
LATROWS = 32
D = 7168
KW = LATENT + 128
CHUNK = 512
PIECE = 1024
HALF = PIECE // 2
PIECES = ("x", "z", "x", "z", "x", "z", "z")
ORDER = (
    (1, 1), (3, 1), (0, 1), (5, 1), (6, 1), (2, 1), (1, 2), (3, 2), (0, 2), (4, 1), (5, 2),
    (1, 3), (6, 2), (3, 3), (2, 2), (0, 3), (5, 3), (4, 2), (6, 3), (2, 3), (4, 3),
)
SCALE2 = 0.135 * math.log2(math.e)

MESH = pl.DeviceIdType.MESH


def device(y, k, a, z, p):
    return (y * 2 + k, a * 4 + z, p)


def turn(v, n):
    return lax.rem(v + n, 4)


def rope_tables():
    f = 10000.0 ** (-(np.arange(32, dtype=np.float64) * 2.0 / ROPE))
    lane_f = np.tile(f, 4)
    sign = np.tile(np.concatenate([-np.ones(32), np.ones(32)]), 2)
    inner = np.arange(BLOCK, dtype=np.float64)[:, None] * lane_f
    outer = np.arange(16, dtype=np.float64)[:, None] * BLOCK * lane_f
    within = np.stack([np.cos(inner), np.sin(inner) * sign]).astype(np.float32)
    blocks = np.stack([np.cos(outer), np.sin(outer) * sign]).astype(np.float32)
    return np.concatenate([within, blocks], axis=1)


def rotation(tables, which, first, count):
    c_in = tables[0, pl.ds(first, count), :]
    s_in = tables[1, pl.ds(first, count), :]
    c_out = tables[0, pl.ds(BLOCK + which, 1), :]
    s_out = tables[1, pl.ds(BLOCK + which, 1), :]
    return c_out * c_in - s_out * s_in, s_out * c_in + c_out * s_in


def swapped(v):
    return jnp.concatenate([v[:, 32:64], v[:, :32], v[:, 96:], v[:, 64:96]], axis=1)


def remote(src, dst, send, recv, to):
    return pltpu.make_async_remote_copy(
        src_ref=src, dst_ref=dst, send_sem=send, recv_sem=recv, device_id=to, device_id_type=MESH
    )


def wide(ref):
    return ref[...].astype(jnp.float32)


def layer_kernel(
    lat_in, gain_in, tables_in, order_in, q_in, up_in, w_in, residual_in,
    out,
    lat, gain, tables, order, q, up_k, up_v, wv, residual,
    kl, q_t, up_vt, key, value_t, bias, top, acc, att,
    part, early, late, crossed, final,
    load_sem, up_sem, w_sem, g_send, g_recv, send, recv,
):
    c = lax.axis_index("ctx")
    t = lax.axis_index("tp")
    p = lax.axis_index("pp")
    y, k, a, z = c // 2, lax.rem(c, 2), t // 4, lax.rem(t, 4)
    z_to = {n: device(y, k, a, turn(z, n), p) for n in (1, 3, 2)}
    y_to = {n: device(turn(y, n), k, a, z, p) for n in (1, 3, 2)}
    x_to = device(y, k, 1 - a, z, p)
    k_to = device(y, 1 - k, a, z, p)
    pp_to = device(y, k, 1 - a, z, 1 - p)

    loads = {}

    def load(name, src, dst, sem):
        made = pltpu.make_async_copy(src, dst, sem)
        made.start()
        loads[name] = made

    load("lat", lat_in.at[0], lat, load_sem.at[0])
    load("order", order_in, order, load_sem.at[1])
    load("gain", gain_in, gain, load_sem.at[2])
    load("tables", tables_in, tables, load_sem.at[3])
    barrier = pltpu.get_barrier_semaphore()
    for to in [*z_to.values(), *y_to.values(), x_to, k_to, pp_to]:
        pl.semaphore_signal(barrier, inc=1, device_id=to, device_id_type=MESH)

    load("q", q_in.at[0], q, load_sem.at[4])
    for h in range(HEADS):
        at = pl.ds(h * VDIM, VDIM)
        load(("k", h), up_in.at[0, :, pl.ds(h * 256, NOPE)], up_k.at[:, at], up_sem.at[h])
        load(("v", h), up_in.at[0, :, pl.ds(h * 256 + NOPE, VDIM)], up_v.at[:, at], up_sem.at[8 + h])
    columns = [pl.ds(j * PIECE, PIECE) for j in range(len(PIECES))]

    for name in ("lat", "order", "gain", "tables"):
        loads[name].wait()
    rows = lat[...].astype(jnp.float32)
    low_rank = rows[:, :LATENT]
    scale = lax.rsqrt(jnp.mean(low_rank * low_rank, axis=-1, keepdims=True) + 1e-6)
    normed = (low_rank * scale * gain[...]).astype(jnp.bfloat16)
    twice = jnp.concatenate([rows[:, LATENT:], rows[:, LATENT:]], axis=1)
    cos, sin = rotation(tables, order[0, c * 2 + a], z * LATROWS, LATROWS)
    roped = ((twice * cos + swapped(twice) * sin) * SCALE2).astype(jnp.bfloat16)
    own = jnp.concatenate([normed, roped], axis=1)
    kl[0, 0, 0, 0, 0] = own[:16]
    kl[0, 1, 0, 0, 0] = own[16:]
    pl.semaphore_wait(barrier, 9)

    sent = []

    def push(src, dst, n, to):
        made = remote(src, dst, g_send.at[n], g_recv.at[n], to)
        made.start()
        sent.append(made)
        return made

    to_x = push(kl.at[0, :, 0, 0, 0], kl.at[0, :, 0, 1, 0], 0, x_to)

    loads["q"].wait()
    lane = lax.broadcasted_iota(jnp.int32, (BLOCK, 128), 1)
    for half in range(2):
        cos, sin = rotation(tables, order[0, c * 2 + half], 0, BLOCK)
        at = pl.ds(half * BLOCK, BLOCK)
        for pair in range(HEADS // 2):
            both = q[at, pair * 384 : (pair + 1) * 384].astype(jnp.float32)
            v = jnp.concatenate([both[:, 128:192], both[:, 320:384]], axis=1)
            turned = v * cos + swapped(v) * sin
            q_t[pair * 2, :NOPE, at] = both[:, :128].T.astype(jnp.bfloat16)
            q_t[pair * 2, NOPE:, at] = jnp.where(lane < ROPE, turned, 0.0).T.astype(jnp.bfloat16)
            q_t[pair * 2 + 1, :NOPE, at] = both[:, 192:320].T.astype(jnp.bfloat16)
            q_t[pair * 2 + 1, NOPE:, at] = jnp.where(lane < ROPE, 0.0, turned).T.astype(jnp.bfloat16)

    to_x.wait_recv()
    near = []
    for i, n in enumerate((1, 3, 2)):
        near.append(push(kl.at[0, 0, 0, :, 0], kl.at[0, 0, 0, :, 4 - n], 1 + i, z_to[n]))
        near.append(push(kl.at[0, 1, 0, :, 0], kl.at[0, 1, 0, :, 4 - n], 4 + i, y_to[n]))
    for h in range(HEADS):
        loads["v", h].wait()
        at = pl.ds(h * VDIM, VDIM)
        up_vt[at, :] = up_v[:, at].astype(jnp.float32).T.astype(jnp.bfloat16)
    for made in near:
        made.wait_recv()
    arrivals = {}
    for i, n in enumerate((3, 1)):
        arrivals[4 - n] = (
            push(kl.at[0, 0, 0], kl.at[4 - n, 0, 0], 7 + i, y_to[n]),
            push(kl.at[0, 1, 0], kl.at[4 - n, 1, 0], 9 + i, z_to[n]),
        )

    def forward(slot):
        side, to = (0, 3) if slot == 1 else (1, 1)
        return (
            push(kl.at[slot, 0, 0, side], kl.at[2, 0, 0, side], 11 + side, y_to[to]),
            push(kl.at[slot, 1, 0, side], kl.at[2, 1, 0, side], 17 + side, z_to[to]),
        )

    def share(slot):
        return push(kl.at[slot, :, 0], kl.at[slot, :, 1], 13 + slot, k_to)

    row = lax.broadcasted_iota(jnp.int32, (BLOCK, BLOCK), 0)
    second = row >= 64
    minor = lax.rem(row, 64) // 16
    deep = lax.rem(row, 16)
    query_in = lax.broadcasted_iota(jnp.int32, (BLOCK, BLOCK), 1)
    query_at = [order[0, c * 2 + n] * BLOCK + query_in for n in range(2)]

    def mask(slot):
        for half in range(2):
            for core in range(2):
                here = k if core == 0 else 1 - k
                if half == 0:
                    there = (turn(y, slot) * 2 + here) * 2
                    block = jnp.where(second, order[0, there + 1 - a], order[0, there + a])
                    key_at = block * BLOCK + lax.rem(minor + z, 4) * LATROWS + deep
                else:
                    block = jnp.zeros_like(row)
                    for m in range(4):
                        there = (turn(y, m) * 2 + here) * 2
                        one = jnp.where(second, order[0, there + 1 - a], order[0, there + a])
                        block = jnp.where(minor == m, one, block)
                    key_at = block * BLOCK + turn(z, slot) * LATROWS + 16 + deep
                for n in range(2):
                    bias[pl.ds((half * 2 + core) * BLOCK, BLOCK), pl.ds(n * BLOCK, BLOCK)] = jnp.where(
                        key_at <= query_at[n], 0.0, -1e30
                    )

    ones = jnp.ones((16, CHUNK), jnp.bfloat16)

    def attend(slot, first, last, between, when):
        latent = kl[slot].reshape(CHUNK, KW)
        low_rank, key_rope = latent[:, :LATENT], latent[:, LATENT:]

        def make_keys(n):
            at = pl.ds(n * 256, 256)
            made = jnp.dot(low_rank, up_k[:, at], preferred_element_type=jnp.float32)
            key[:, at] = (made * SCALE2).astype(jnp.bfloat16)

        def make_values(n):
            at = pl.ds(n * 256, 256)
            value_t[at, :] = lax.dot_general(
                up_vt[at, :], low_rank, (((1,), (1,)), ((), ())), preferred_element_type=jnp.float32
            ).astype(jnp.bfloat16)

        def score(h):
            keys = jnp.concatenate([key[:, pl.ds(h * VDIM, VDIM)], key_rope], axis=1)
            return jnp.dot(keys, q_t[h], preferred_element_type=jnp.float32) + bias[...]

        def soften(h, scores):
            high = jnp.max(scores, axis=0, keepdims=True)
            shrink = None
            if not first:
                before = top[h, :1]
                high = jnp.maximum(before, high)
                shrink = jnp.exp2(before - high)
            if not last:
                top[h] = jnp.broadcast_to(high, (8, ROWS))
            return jnp.exp2(scores - high).astype(jnp.bfloat16), shrink

        def gather_values(h, weights, shrink):
            at = pl.ds(h * VDIM, VDIM)
            values = jnp.concatenate([value_t[at, :], ones], axis=0)
            summed = jnp.dot(values, weights, preferred_element_type=jnp.float32)
            if not first:
                summed = summed + acc[h] * shrink
            if last:
                att[:, at] = (summed[:VDIM] / summed[VDIM : VDIM + 1]).T.astype(jnp.bfloat16)
            else:
                acc[h] = summed

        make_keys(0)
        mask(slot)
        make_values(0)
        scores, waiting = score(0), None
        for h in range(HEADS):
            if h == when:
                between()
            more = h % 2 == 0 and h < 6
            if more:
                make_keys(h // 2 + 1)
            following = score(h + 1) if h < HEADS - 1 else None
            weights, shrink = soften(h, scores)
            if more:
                make_values(h // 2 + 1)
            if waiting:
                gather_values(*waiting)
            waiting, scores = (h, weights, shrink), following
        gather_values(*waiting)

    def landed_slot(slot):
        for made in arrivals[slot]:
            made.wait_recv()

    shared = {0: share(0)}

    def pass_on(*slots):
        if slots == (1, 3):
            landed_slot(1)
            ahead = forward(1)
            landed_slot(3)
            arrivals[2] = ahead + forward(3)
        else:
            landed_slot(2)
        for slot in slots:
            shared[slot] = share(slot)

    for h in range(HEADS):
        loads["k", h].wait()
    shared[0].wait_recv()
    load("residual", residual_in.at[0], residual, load_sem.at[5])
    for j in range(len(PIECES)):
        load(("w", j), w_in.at[0, :, columns[j]], wv.at[j], w_sem.at[j])
    attend(0, True, False, lambda: pass_on(1, 3), 5)
    shared[1].wait_recv()
    attend(1, False, False, lambda: pass_on(2), 7)
    shared[3].wait_recv()
    attend(3, False, False, lambda: None, 5)
    shared[2].wait_recv()
    attend(2, False, True, lambda: None, 5)

    above, below, far = turn(z, 1), turn(z, 3), turn(z, 2)
    left, right = pl.ds(0, HALF), pl.ds(HALF, HALF)
    copies = {}

    def copy(src, dst, j, n, to):
        made = remote(src, dst, send.at[j, n], recv.at[j, n], to)
        made.start()
        sent.append(made)
        copies[j, n] = made

    def own_residual(j):
        return residual[:, columns[j]].astype(jnp.float32)

    def spread(j, side):
        copy(part.at[j, side, far, :, left], early.at[j, 0, side], j, 0, z_to[1])
        copy(part.at[j, side, far, :, right], early.at[j, 1, side], j, 1, z_to[3])
        copy(part.at[j, side, above, :, right], late.at[j, 0, side, :, right], j, 2, z_to[1])
        copy(part.at[j, side, below, :, left], late.at[j, 1, side, :, left], j, 3, z_to[3])

    def relay(j, side):
        copies[j, 0].wait_recv()
        mine = part.at[j, side, above, :, left]
        mine[...] = (wide(mine) + wide(early.at[j, 0, side])).astype(jnp.bfloat16)
        copy(mine, late.at[j, 0, side, :, left], j, 4, z_to[1])
        copies[j, 1].wait_recv()
        mine = part.at[j, side, below, :, right]
        mine[...] = (wide(mine) + wide(early.at[j, 1, side])).astype(jnp.bfloat16)
        copy(mine, late.at[j, 1, side, :, right], j, 5, z_to[3])

    def landed(j):
        for n in (2, 3, 4, 5):
            copies[j, n].wait_recv()

    def ring_sum(j, side):
        return wide(part.at[j, side, z]) + wide(late.at[j, 0, side]) + wide(late.at[j, 1, side])

    def finish(j, value):
        final[j] = value.astype(jnp.bfloat16)
        copy(final.at[j], out.at[0, :, columns[j]], j, 7, pp_to)

    def product(j):
        loads["w", j].wait()
        made = jnp.dot(att[...], wv[j], preferred_element_type=jnp.float32)
        part[j] = made.astype(jnp.bfloat16).reshape(2, 4, LATROWS, PIECE)

    def z_step(j, step):
        if step == 0:
            product(j)
            spread(j, slice(None))
        elif step == 1:
            relay(j, slice(None))
        elif step == 2:
            landed(j)
            part[j, a, z] = (ring_sum(j, a) + own_residual(j)).astype(jnp.bfloat16)
            copy(part.at[j, a, z], crossed.at[j, 0], j, 6, x_to)
        elif step == 3:
            copies[j, 6].wait_recv()
            finish(j, ring_sum(j, 1 - a) + wide(crossed.at[j, 0]))

    def x_step(j, step):
        if step == 0:
            product(j)
            part[j, a, z] = (wide(part.at[j, a, z]) + own_residual(j)).astype(jnp.bfloat16)
            copy(part.at[j, a], crossed.at[j], j, 6, x_to)
        elif step == 1:
            copies[j, 6].wait_recv()
            part[j, 1 - a] = (wide(part.at[j, 1 - a]) + wide(crossed.at[j])).astype(jnp.bfloat16)
            spread(j, 1 - a)
        elif step == 2:
            relay(j, 1 - a)
        elif step == 3:
            landed(j)
            finish(j, ring_sum(j, 1 - a))

    steps = {"z": z_step, "x": x_step}
    loads["residual"].wait()
    for j, kind in enumerate(PIECES):
        steps[kind](j, 0)
    for j, step in ORDER:
        steps[PIECES[j]](j, step)
    for j in range(len(PIECES)):
        copies[j, 7].wait_recv()
    for made in sent:
        made.wait_send()


def local(queries, latents, latent_gain, w_ukv, w_o, residual, block_order):
    n = len(PIECES)
    hbm = pl.BlockSpec(memory_space=pltpu.HBM)
    bf16, f32 = jnp.bfloat16, jnp.float32
    dma = pltpu.SemaphoreType.DMA
    return pl.pallas_call(
        layer_kernel,
        out_shape=jax.ShapeDtypeStruct((1, LATROWS, D), bf16),
        in_specs=[hbm] * 8,
        out_specs=pl.BlockSpec(memory_space=pltpu.VMEM),
        scratch_shapes=[
            pltpu.VMEM((LATROWS, LATENT + ROPE), bf16),
            pltpu.VMEM((1, LATENT), f32),
            pltpu.VMEM((2, BLOCK + 16, 128), f32),
            pltpu.SMEM((1, 16), jnp.int32),
            pltpu.VMEM((ROWS, HEADS * (NOPE + ROPE)), bf16),
            pltpu.VMEM((LATENT, HEADS * NOPE), bf16),
            pltpu.VMEM((LATENT, HEADS * VDIM), bf16),
            pltpu.VMEM((n, HEADS * VDIM, PIECE), bf16),
            pltpu.VMEM((LATROWS, D), bf16),
            pltpu.VMEM((4, 2, 2, 2, 4, 16, KW), bf16),
            pltpu.VMEM((HEADS, 256, ROWS), bf16),
            pltpu.VMEM((HEADS * VDIM, LATENT), bf16),
            pltpu.VMEM((CHUNK, HEADS * NOPE), bf16),
            pltpu.VMEM((HEADS * VDIM, CHUNK), bf16),
            pltpu.VMEM((CHUNK, ROWS), f32),
            pltpu.VMEM((HEADS, 8, ROWS), f32),
            pltpu.VMEM((HEADS, VDIM + 16, ROWS), f32),
            pltpu.VMEM((ROWS, HEADS * VDIM), bf16),
            pltpu.VMEM((n, 2, 4, LATROWS, PIECE), bf16),
            pltpu.VMEM((n, 2, 2, LATROWS, HALF), bf16),
            pltpu.VMEM((n, 2, 2, LATROWS, PIECE), bf16),
            pltpu.VMEM((n, 4, LATROWS, PIECE), bf16),
            pltpu.VMEM((n, LATROWS, PIECE), bf16),
            dma((6,)),
            dma((2 * HEADS,)),
            dma((n,)),
            dma((19,)),
            dma((19,)),
            dma((n, 8)),
            dma((n, 8)),
        ],
        compiler_params=pltpu.CompilerParams(
            collective_id=0, has_side_effects=True, vmem_limit_bytes=58 * 2**20
        ),
        name="layer",
    )(latents, latent_gain, jnp.asarray(rope_tables()), block_order, queries, w_ukv, w_o, residual)


def solution(mesh):
    in_specs = (
        P("pp", "ctx", "tp"),
        P("pp", ("ctx", "tp"), None),
        P("pp", None),
        P("pp", None, "tp"),
        P("pp", "tp", None),
        P("pp", ("ctx", "tp"), None),
        P("pp", None),
    )
    out_specs = P("pp", ("ctx", "tp"), None)
    return jax.shard_map(local, mesh=mesh, in_specs=in_specs, out_specs=out_specs, check_vma=False)
```

```python
import math

import jax
import jax.numpy as jnp
import numpy as np
from jax import lax
from jax.experimental import pallas as pl
from jax.experimental.pallas import tpu as pltpu
from jax.sharding import PartitionSpec as P

NOPE = 128
ROPE = 64
VDIM = 128
LATENT = 512
BLOCK = 128
HEADS = 8
ROWS = 256
LATROWS = 32
D = 7168
KW = LATENT + 128
CHUNK = 512
PIECES = (("x", 512), ("z", 512), ("z", 512), ("z", 512), ("x", 512), ("z", 512), ("z", 1024), ("z", 1024), ("x", 1024), ("x", 1024))
ORDER = (
    (1, 1), (2, 1), (0, 1), (3, 1), (5, 1), (4, 1), (6, 1), (7, 1), (8, 1), (1, 2),
    (2, 2), (0, 2), (3, 2), (5, 2), (4, 2), (9, 1), (6, 2), (1, 3), (2, 3), (7, 2),
    (3, 3), (8, 2), (5, 3), (0, 3), (4, 3), (6, 3), (9, 2), (7, 3), (8, 3), (9, 3),
)
WIDEST = max(width for _, width in PIECES)
SCALE2 = 0.135 * math.log2(math.e)

MESH = pl.DeviceIdType.MESH


def device(y, k, a, z, p):
    return (y * 2 + k, a * 4 + z, p)


def turn(v, n):
    return lax.rem(v + n, 4)


def rope_tables():
    f = 10000.0 ** (-(np.arange(32, dtype=np.float64) * 2.0 / ROPE))
    lane_f = np.tile(f, 4)
    sign = np.tile(np.concatenate([-np.ones(32), np.ones(32)]), 2)
    inner = np.arange(BLOCK, dtype=np.float64)[:, None] * lane_f
    outer = np.arange(16, dtype=np.float64)[:, None] * BLOCK * lane_f
    within = np.stack([np.cos(inner), np.sin(inner) * sign]).astype(np.float32)
    blocks = np.stack([np.cos(outer), np.sin(outer) * sign]).astype(np.float32)
    return np.concatenate([within, blocks], axis=1)


def rotation(tables, which, first, count):
    c_in = tables[0, pl.ds(first, count), :]
    s_in = tables[1, pl.ds(first, count), :]
    c_out = tables[0, pl.ds(BLOCK + which, 1), :]
    s_out = tables[1, pl.ds(BLOCK + which, 1), :]
    return c_out * c_in - s_out * s_in, s_out * c_in + c_out * s_in


def swapped(v):
    return jnp.concatenate([v[:, 32:64], v[:, :32], v[:, 96:], v[:, 64:96]], axis=1)


def remote(src, dst, send, recv, to):
    return pltpu.make_async_remote_copy(
        src_ref=src, dst_ref=dst, send_sem=send, recv_sem=recv, device_id=to, device_id_type=MESH
    )


def wide(ref):
    return ref[...].astype(jnp.float32)


def layer_kernel(
    lat_in, gain_in, tables_in, order_in, q_in, up_in, w_in, residual_in,
    out,
    lat, gain, tables, order, q, up_k, up_v, wv, residual,
    kl, q_t, up_vt, key, value_t, bias, top, acc, att,
    part, early, late, crossed, final,
    load_sem, up_sem, w_sem, g_send, g_recv, send, recv,
):
    c = lax.axis_index("ctx")
    t = lax.axis_index("tp")
    p = lax.axis_index("pp")
    y, k, a, z = c // 2, lax.rem(c, 2), t // 4, lax.rem(t, 4)
    z_to = {n: device(y, k, a, turn(z, n), p) for n in (1, 3, 2)}
    y_to = {n: device(turn(y, n), k, a, z, p) for n in (1, 3, 2)}
    x_to = device(y, k, 1 - a, z, p)
    k_to = device(y, 1 - k, a, z, p)
    pp_to = device(y, k, 1 - a, z, 1 - p)

    loads = {}

    def load(name, src, dst, sem):
        made = pltpu.make_async_copy(src, dst, sem)
        made.start()
        loads[name] = made

    load("lat", lat_in.at[0], lat, load_sem.at[0])
    load("order", order_in, order, load_sem.at[1])
    load("gain", gain_in, gain, load_sem.at[2])
    load("tables", tables_in, tables, load_sem.at[3])
    barrier = pltpu.get_barrier_semaphore()
    for to in [*z_to.values(), *y_to.values(), x_to, k_to, pp_to]:
        pl.semaphore_signal(barrier, inc=1, device_id=to, device_id_type=MESH)

    load("q", q_in.at[0], q, load_sem.at[4])
    for h in range(HEADS):
        at = pl.ds(h * VDIM, VDIM)
        load(("k", h), up_in.at[0, :, pl.ds(h * 256, NOPE)], up_k.at[:, at], up_sem.at[h])
        load(("v", h), up_in.at[0, :, pl.ds(h * 256 + NOPE, VDIM)], up_v.at[:, at], up_sem.at[8 + h])
    widths = [width for _, width in PIECES]
    columns = [pl.ds(sum(widths[:j]), widths[j]) for j in range(len(PIECES))]
    full = [pl.ds(0, width) for width in widths]
    left = [pl.ds(0, width // 2) for width in widths]
    right = [pl.ds(width // 2, width // 2) for width in widths]

    for name in ("lat", "order", "gain", "tables"):
        loads[name].wait()
    rows = lat[...].astype(jnp.float32)
    low_rank = rows[:, :LATENT]
    scale = lax.rsqrt(jnp.mean(low_rank * low_rank, axis=-1, keepdims=True) + 1e-6)
    normed = (low_rank * scale * gain[...]).astype(jnp.bfloat16)
    twice = jnp.concatenate([rows[:, LATENT:], rows[:, LATENT:]], axis=1)
    cos, sin = rotation(tables, order[0, c * 2 + a], z * LATROWS, LATROWS)
    roped = ((twice * cos + swapped(twice) * sin) * SCALE2).astype(jnp.bfloat16)
    own = jnp.concatenate([normed, roped], axis=1)
    kl[0, 0, 0, 0, 0] = own[:16]
    kl[0, 1, 0, 0, 0] = own[16:]
    pl.semaphore_wait(barrier, 9)

    sent = []

    def push(src, dst, n, to):
        made = remote(src, dst, g_send.at[n], g_recv.at[n], to)
        made.start()
        sent.append(made)
        return made

    to_x = push(kl.at[0, :, 0, 0, 0], kl.at[0, :, 0, 1, 0], 0, x_to)

    loads["q"].wait()
    lane = lax.broadcasted_iota(jnp.int32, (BLOCK, 128), 1)
    for half in range(2):
        cos, sin = rotation(tables, order[0, c * 2 + half], 0, BLOCK)
        at = pl.ds(half * BLOCK, BLOCK)
        for pair in range(HEADS // 2):
            both = q[at, pair * 384 : (pair + 1) * 384].astype(jnp.float32)
            v = jnp.concatenate([both[:, 128:192], both[:, 320:384]], axis=1)
            turned = v * cos + swapped(v) * sin
            q_t[pair * 2, :NOPE, at] = both[:, :128].T.astype(jnp.bfloat16)
            q_t[pair * 2, NOPE:, at] = jnp.where(lane < ROPE, turned, 0.0).T.astype(jnp.bfloat16)
            q_t[pair * 2 + 1, :NOPE, at] = both[:, 192:320].T.astype(jnp.bfloat16)
            q_t[pair * 2 + 1, NOPE:, at] = jnp.where(lane < ROPE, 0.0, turned).T.astype(jnp.bfloat16)

    to_x.wait_recv()
    near = []
    for i, n in enumerate((1, 3, 2)):
        near.append(push(kl.at[0, 0, 0, :, 0], kl.at[0, 0, 0, :, 4 - n], 1 + i, z_to[n]))
        near.append(push(kl.at[0, 1, 0, :, 0], kl.at[0, 1, 0, :, 4 - n], 4 + i, y_to[n]))
    for h in range(HEADS):
        loads["v", h].wait()
        at = pl.ds(h * VDIM, VDIM)
        up_vt[at, :] = up_v[:, at].astype(jnp.float32).T.astype(jnp.bfloat16)
    for made in near:
        made.wait_recv()
    arrivals = {}
    for i, n in enumerate((3, 1)):
        arrivals[4 - n] = (
            push(kl.at[0, 0, 0], kl.at[4 - n, 0, 0], 7 + i, y_to[n]),
            push(kl.at[0, 1, 0], kl.at[4 - n, 1, 0], 9 + i, z_to[n]),
        )

    def forward(slot):
        side, to = (0, 3) if slot == 1 else (1, 1)
        return (
            push(kl.at[slot, 0, 0, side], kl.at[2, 0, 0, side], 11 + side, y_to[to]),
            push(kl.at[slot, 1, 0, side], kl.at[2, 1, 0, side], 17 + side, z_to[to]),
        )

    def share(slot):
        return push(kl.at[slot, :, 0], kl.at[slot, :, 1], 13 + slot, k_to)

    row = lax.broadcasted_iota(jnp.int32, (BLOCK, BLOCK), 0)
    second = row >= 64
    minor = lax.rem(row, 64) // 16
    deep = lax.rem(row, 16)
    query_in = lax.broadcasted_iota(jnp.int32, (BLOCK, BLOCK), 1)
    query_at = [order[0, c * 2 + n] * BLOCK + query_in for n in range(2)]

    def mask(slot):
        for half in range(2):
            for core in range(2):
                here = k if core == 0 else 1 - k
                if half == 0:
                    there = (turn(y, slot) * 2 + here) * 2
                    block = jnp.where(second, order[0, there + 1 - a], order[0, there + a])
                    key_at = block * BLOCK + lax.rem(minor + z, 4) * LATROWS + deep
                else:
                    block = jnp.zeros_like(row)
                    for m in range(4):
                        there = (turn(y, m) * 2 + here) * 2
                        one = jnp.where(second, order[0, there + 1 - a], order[0, there + a])
                        block = jnp.where(minor == m, one, block)
                    key_at = block * BLOCK + turn(z, slot) * LATROWS + 16 + deep
                for n in range(2):
                    bias[pl.ds((half * 2 + core) * BLOCK, BLOCK), pl.ds(n * BLOCK, BLOCK)] = jnp.where(
                        key_at <= query_at[n], 0.0, -1e30
                    )

    ones = jnp.ones((16, CHUNK), jnp.bfloat16)

    def attend(slot, first, last, between, when):
        latent = kl[slot].reshape(CHUNK, KW)
        low_rank, key_rope = latent[:, :LATENT], latent[:, LATENT:]

        def make_keys(n):
            at = pl.ds(n * 256, 256)
            made = jnp.dot(low_rank, up_k[:, at], preferred_element_type=jnp.float32)
            key[:, at] = (made * SCALE2).astype(jnp.bfloat16)

        def make_values(n):
            at = pl.ds(n * 256, 256)
            value_t[at, :] = lax.dot_general(
                up_vt[at, :], low_rank, (((1,), (1,)), ((), ())), preferred_element_type=jnp.float32
            ).astype(jnp.bfloat16)

        def score(h):
            keys = jnp.concatenate([key[:, pl.ds(h * VDIM, VDIM)], key_rope], axis=1)
            return jnp.dot(keys, q_t[h], preferred_element_type=jnp.float32) + bias[...]

        def soften(h, scores):
            high = jnp.max(scores, axis=0, keepdims=True)
            shrink = None
            if not first:
                before = top[h, :1]
                high = jnp.maximum(before, high)
                shrink = jnp.exp2(before - high)
            if not last:
                top[h] = jnp.broadcast_to(high, (8, ROWS))
            return jnp.exp2(scores - high).astype(jnp.bfloat16), shrink

        def gather_values(h, weights, shrink):
            at = pl.ds(h * VDIM, VDIM)
            values = jnp.concatenate([value_t[at, :], ones], axis=0)
            summed = jnp.dot(values, weights, preferred_element_type=jnp.float32)
            if not first:
                summed = summed + acc[h] * shrink
            if last:
                att[:, at] = (summed[:VDIM] / summed[VDIM : VDIM + 1]).T.astype(jnp.bfloat16)
            else:
                acc[h] = summed

        make_keys(0)
        mask(slot)
        make_values(0)
        scores, waiting = score(0), None
        for h in range(HEADS):
            if h == when:
                between()
            more = h % 2 == 0 and h < 6
            if more:
                make_keys(h // 2 + 1)
            following = score(h + 1) if h < HEADS - 1 else None
            weights, shrink = soften(h, scores)
            if more:
                make_values(h // 2 + 1)
            if waiting:
                gather_values(*waiting)
            waiting, scores = (h, weights, shrink), following
        gather_values(*waiting)

    def landed_slot(slot):
        for made in arrivals[slot]:
            made.wait_recv()

    shared = {0: share(0)}

    def pass_on(*slots):
        if slots == (1, 3):
            landed_slot(1)
            ahead = forward(1)
            landed_slot(3)
            arrivals[2] = ahead + forward(3)
        else:
            landed_slot(2)
        for slot in slots:
            shared[slot] = share(slot)

    for h in range(HEADS):
        loads["k", h].wait()
    shared[0].wait_recv()
    load("residual", residual_in.at[0], residual, load_sem.at[5])
    for j in range(len(PIECES)):
        load(("w", j), w_in.at[0, :, columns[j]], wv.at[:, columns[j]], w_sem.at[j])
    attend(0, True, False, lambda: pass_on(1, 3), 5)
    shared[1].wait_recv()
    attend(1, False, False, lambda: pass_on(2), 7)
    shared[3].wait_recv()
    attend(3, False, False, lambda: None, 5)
    shared[2].wait_recv()
    attend(2, False, True, lambda: None, 5)

    above, below, far = turn(z, 1), turn(z, 3), turn(z, 2)
    copies = {}

    def copy(src, dst, j, n, to):
        made = remote(src, dst, send.at[j, n], recv.at[j, n], to)
        made.start()
        sent.append(made)
        copies[j, n] = made

    def own_residual(j):
        return residual[:, columns[j]].astype(jnp.float32)

    def spread(j, side):
        copy(part.at[j, side, far, :, left[j]], early.at[j, 0, side, :, left[j]], j, 0, z_to[1])
        copy(part.at[j, side, far, :, right[j]], early.at[j, 1, side, :, left[j]], j, 1, z_to[3])
        copy(part.at[j, side, above, :, right[j]], late.at[j, 0, side, :, right[j]], j, 2, z_to[1])
        copy(part.at[j, side, below, :, left[j]], late.at[j, 1, side, :, left[j]], j, 3, z_to[3])

    def relay(j, side):
        copies[j, 0].wait_recv()
        mine = part.at[j, side, above, :, left[j]]
        mine[...] = (wide(mine) + wide(early.at[j, 0, side, :, left[j]])).astype(jnp.bfloat16)
        copy(mine, late.at[j, 0, side, :, left[j]], j, 4, z_to[1])
        copies[j, 1].wait_recv()
        mine = part.at[j, side, below, :, right[j]]
        mine[...] = (wide(mine) + wide(early.at[j, 1, side, :, left[j]])).astype(jnp.bfloat16)
        copy(mine, late.at[j, 1, side, :, right[j]], j, 5, z_to[3])

    def landed(j):
        for n in (2, 3, 4, 5):
            copies[j, n].wait_recv()

    def ring_sum(j, side):
        here = wide(part.at[j, side, z, :, full[j]])
        return here + wide(late.at[j, 0, side, :, full[j]]) + wide(late.at[j, 1, side, :, full[j]])

    def finish(j, value):
        final[j, :, full[j]] = value.astype(jnp.bfloat16)
        copy(final.at[j, :, full[j]], out.at[0, :, columns[j]], j, 7, pp_to)

    def product(j):
        loads["w", j].wait()
        made = jnp.dot(att[...], wv[:, columns[j]], preferred_element_type=jnp.float32)
        part[j, :, :, :, full[j]] = made.astype(jnp.bfloat16).reshape(2, 4, LATROWS, widths[j])

    def z_step(j, step):
        mine = part.at[j, a, z, :, full[j]]
        crossing = crossed.at[j, 0, :, full[j]]
        if step == 0:
            product(j)
            spread(j, slice(None))
        elif step == 1:
            relay(j, slice(None))
        elif step == 2:
            landed(j)
            mine[...] = (ring_sum(j, a) + own_residual(j)).astype(jnp.bfloat16)
            copy(mine, crossing, j, 6, x_to)
        elif step == 3:
            copies[j, 6].wait_recv()
            finish(j, ring_sum(j, 1 - a) + wide(crossing))

    def x_step(j, step):
        mine = part.at[j, a, z, :, full[j]]
        kept = part.at[j, 1 - a, :, :, full[j]]
        crossing = crossed.at[j, :, :, full[j]]
        if step == 0:
            product(j)
            mine[...] = (wide(mine) + own_residual(j)).astype(jnp.bfloat16)
            copy(part.at[j, a, :, :, full[j]], crossing, j, 6, x_to)
        elif step == 1:
            copies[j, 6].wait_recv()
            kept[...] = (wide(kept) + wide(crossing)).astype(jnp.bfloat16)
            spread(j, 1 - a)
        elif step == 2:
            relay(j, 1 - a)
        elif step == 3:
            landed(j)
            finish(j, ring_sum(j, 1 - a))

    steps = {"z": z_step, "x": x_step}
    loads["residual"].wait()
    for j, (kind, _) in enumerate(PIECES):
        steps[kind](j, 0)
    for j, step in ORDER:
        steps[PIECES[j][0]](j, step)
    for j in range(len(PIECES)):
        copies[j, 7].wait_recv()
    for made in sent:
        made.wait_send()


def local(queries, latents, latent_gain, w_ukv, w_o, residual, block_order):
    n = len(PIECES)
    hbm = pl.BlockSpec(memory_space=pltpu.HBM)
    bf16, f32 = jnp.bfloat16, jnp.float32
    dma = pltpu.SemaphoreType.DMA
    return pl.pallas_call(
        layer_kernel,
        out_shape=jax.ShapeDtypeStruct((1, LATROWS, D), bf16),
        in_specs=[hbm] * 8,
        out_specs=pl.BlockSpec(memory_space=pltpu.VMEM),
        scratch_shapes=[
            pltpu.VMEM((LATROWS, LATENT + ROPE), bf16),
            pltpu.VMEM((1, LATENT), f32),
            pltpu.VMEM((2, BLOCK + 16, 128), f32),
            pltpu.SMEM((1, 16), jnp.int32),
            pltpu.VMEM((ROWS, HEADS * (NOPE + ROPE)), bf16),
            pltpu.VMEM((LATENT, HEADS * NOPE), bf16),
            pltpu.VMEM((LATENT, HEADS * VDIM), bf16),
            pltpu.VMEM((HEADS * VDIM, D), bf16),
            pltpu.VMEM((LATROWS, D), bf16),
            pltpu.VMEM((4, 2, 2, 2, 4, 16, KW), bf16),
            pltpu.VMEM((HEADS, 256, ROWS), bf16),
            pltpu.VMEM((HEADS * VDIM, LATENT), bf16),
            pltpu.VMEM((CHUNK, HEADS * NOPE), bf16),
            pltpu.VMEM((HEADS * VDIM, CHUNK), bf16),
            pltpu.VMEM((CHUNK, ROWS), f32),
            pltpu.VMEM((HEADS, 8, ROWS), f32),
            pltpu.VMEM((HEADS, VDIM + 16, ROWS), f32),
            pltpu.VMEM((ROWS, HEADS * VDIM), bf16),
            pltpu.VMEM((n, 2, 4, LATROWS, WIDEST), bf16),
            pltpu.VMEM((n, 2, 2, LATROWS, WIDEST // 2), bf16),
            pltpu.VMEM((n, 2, 2, LATROWS, WIDEST), bf16),
            pltpu.VMEM((n, 4, LATROWS, WIDEST), bf16),
            pltpu.VMEM((n, LATROWS, WIDEST), bf16),
            dma((6,)),
            dma((2 * HEADS,)),
            dma((n,)),
            dma((19,)),
            dma((19,)),
            dma((n, 8)),
            dma((n, 8)),
        ],
        compiler_params=pltpu.CompilerParams(
            collective_id=0, has_side_effects=True, vmem_limit_bytes=58 * 2**20
        ),
        name="layer",
    )(latents, latent_gain, jnp.asarray(rope_tables()), block_order, queries, w_ukv, w_o, residual)


def solution(mesh):
    in_specs = (
        P("pp", "ctx", "tp"),
        P("pp", ("ctx", "tp"), None),
        P("pp", None),
        P("pp", None, "tp"),
        P("pp", "tp", None),
        P("pp", ("ctx", "tp"), None),
        P("pp", None),
    )
    out_specs = P("pp", ("ctx", "tp"), None)
    return jax.shard_map(local, mesh=mesh, in_specs=in_specs, out_specs=out_specs, check_vma=False)
```
